256 devices in a mesh: row: 8 (over x, y_lo), col: 32 (over y_hi, z, core).
Axes of the slice: x: 4, y: 4 (y_hi: 2, y_lo: 2; y = y_hi * 2 + y_lo), z: 8, core: 2. Of those that a mesh axis runs over, the one named last changes fastest.
Arguments:
- g_start: float32 [4096, 32768], P('row', 'col'), may hold values from -6 to 6
- cotangent: float32 [4096, 32768], P('row', 'col'), may hold values from -6 to 6
- damping: float32 [32768], replicated, may hold values from 0.1 to 3
- hopping: float32 [6, 32768], replicated, may hold values from -4 to 4
- bonds: int32 [7, 32768], replicated, may hold values 0 or 1
- source: float32 [7, 32768], replicated, may hold values from -5 to 5
Outputs:
- g_end: float32 [4096, 32768], P('row', 'col')
- g_adjoint: float32 [4096, 32768], P('row', 'col')
The draws below stay inside these ranges and needn't reach their ends.
All inputs are finite; a program needn't handle non-finite values.
Results may differ from the reference program's by a relative error of at most 0.00002.
Values sent between devices are 32-bit elements; how exact they have to be, the bound alone decides.
A program may use at most 128 MiB of HBM per device.

```python
import math
import jax
import jax.numpy as jnp

LX = 128
BANDS = 7
MODES = 32768
ROWS = 4096


def touch_ends(drawn, stream_key, low, high):
    index_at = [jax.random.randint(jax.random.fold_in(stream_key, axis), (), 0, length) for axis, length in enumerate(drawn.shape)]
    main_axis = drawn.shape.index(max(drawn.shape))
    neighbour = index_at[:main_axis] + [(index_at[main_axis] + 1) % drawn.shape[main_axis]] + index_at[main_axis + 1:]
    return drawn.at[tuple(index_at)].set(low).at[tuple(neighbour)].set(high)


def levels(key, shape, pieces, low, largest):
    def one(dim, parts):
        steps = jax.random.uniform(jax.random.fold_in(jax.random.fold_in(key, 6), dim), (parts,), jnp.float32, low / len(pieces), largest / len(pieces))
        return jnp.repeat(jnp.exp(steps), shape[dim] // parts).reshape((-1,) + (1,) * (len(shape) - dim - 1))

    factor_of = one(*pieces[0])
    for cut in pieces[1:]:
        factor_of = factor_of * one(*cut)
    return factor_of


def normal_values(rng, shape, scale, most, split=(), kind=jnp.bfloat16):
    values = scale * jax.random.normal(rng, shape, jnp.float32)
    if split:
        values = values * levels(rng, shape, split, -0.22, 0.18)
    return jnp.clip(values, -most, most).astype(kind)


def setup_inputs(seed: int = 0) -> dict:
    arg_keys = jax.random.split(jax.random.key(seed), 7)
    g_start = normal_values(arg_keys[0], (ROWS, MODES), 1.0, 6.0, ((0, 8), (1, 32)), jnp.float32)
    cotangent = normal_values(arg_keys[1], (ROWS, MODES), 1.0, 6.0, ((0, 8), (1, 32)), jnp.float32)
    damping = jnp.clip(jnp.exp(jax.random.uniform(arg_keys[2], (MODES,), jnp.float32, math.log(0.1), math.log(3.0))), 0.1, 3.0)
    hopping = normal_values(arg_keys[3], (BANDS - 1, MODES), 1.0, 4.0, (), jnp.float32)
    bonds = touch_ends((jax.random.randint(arg_keys[4], (BANDS, MODES), 0, 4) < 3).astype(jnp.int32), jax.random.fold_in(arg_keys[4], 1), 0, 1)
    source = normal_values(arg_keys[5], (BANDS, MODES), 1.0, 5.0, (), jnp.float32)
    return {"g_start": g_start, "cotangent": cotangent, "damping": damping, "hopping": hopping, "bonds": bonds, "source": source}


DT = 0.1


def band_offsets(side):
    return (0, 1, -1, 2, -2, 2 * side, -2 * side)


def row_shift(field, offset):
    count = field.shape[1]
    if offset > 0:
        return jnp.concatenate([field[offset:], jnp.zeros((offset, count), jnp.float32)], axis=0)
    if offset < 0:
        return jnp.concatenate([jnp.zeros((-offset, count), jnp.float32), field[:offset]], axis=0)
    return field


def forward_rate(field, coef, source):
    rows = field.shape[0]
    modes = field.shape[1]
    row_ids = jnp.arange(rows, dtype=jnp.int32)
    total = jnp.zeros(field.shape, jnp.float32)
    for index, offset in enumerate(band_offsets(LX)):
        total = total + coef[index, :rows][:, None] * row_shift(field, offset)
        total = total + jnp.roll(field, -offset, axis=1) * coef[index][None, :]
        total = total.at[row_ids, jnp.mod(row_ids + offset, modes).astype(jnp.int32)].add(source[index, :rows])
    return total


def adjoint_rate(field, coef):
    rows = field.shape[0]
    total = jnp.zeros(field.shape, jnp.float32)
    for index, offset in enumerate(band_offsets(LX)):
        total = total + row_shift(coef[index, :rows][:, None] * field, -offset)
        total = total + jnp.roll(field * coef[index][None, :], offset, axis=1)
    return total


def reference(g_start, cotangent, damping, hopping, bonds, source):
    coef = jnp.concatenate([-damping[None, :], hopping], axis=0) * bonds.astype(jnp.float32)
    g_middle = g_start + 0.5 * DT * forward_rate(g_start, coef, source)
    g_end = g_start + DT * forward_rate(g_middle, coef, source)
    c_middle = cotangent + 0.5 * DT * adjoint_rate(cotangent, coef)
    g_adjoint = cotangent + DT * adjoint_rate(c_middle, coef)
    return g_end, g_adjoint
```

```python
import functools

import jax
import jax.numpy as jnp
from jax import lax
from jax.experimental import pallas as pl
from jax.experimental.pallas import tpu as pltpu
from jax.sharding import PartitionSpec as P

LX = 128
DT = 0.1
MESH = pl.DeviceIdType.MESH
STEPS = 8
AHEAD = 3
CHUNK = 32
LANES = 128


def band_offsets(side):
    return (0, 1, -1, 2, -2, 2 * side, -2 * side)


MIRROR = (0, 2, 1, 4, 3, 6, 5)


def kernel(
    tile,
    n_rows,
    n_cols,
    group,
    g_hbm,
    c_hbm,
    row_tab,
    col_tab,
    g_out,
    c_out,
    ext,
    mid,
    fin,
    row_coef,
    load_sem,
    store_sem,
    send_sem,
    recv_sem,
):
    T = tile
    offsets = band_offsets(T // 2)
    r = lax.axis_index("row")
    c = lax.axis_index("col")
    odd = lax.rem(r, 2)
    even = 1 - odd
    partner = r + 1 - 2 * odd
    other = r - 1 + 2 * odd
    has_b = jnp.logical_and(other >= 0, other < n_rows)
    fwd_row = r + 2 - 4 * odd
    has_fwd = jnp.logical_and(fwd_row >= 0, fwd_row < n_rows)
    src_row = r - 2 + 4 * odd
    left = lax.rem(c + n_cols - 1, n_cols)
    right = lax.rem(c + 1, n_cols)
    left_edge = lax.rem(c, group) == 0
    right_edge = lax.rem(c, group) == group - 1
    sides = ((left, left_edge), (right, right_edge))

    a_heavy = odd * T + even * 4 * T
    a_light = even * 5 * T
    b_heavy = odd * 4 * T + even * T
    b_light = odd * 5 * T
    a_mid = a_heavy - T
    b_mid = b_heavy - T
    own_a = 2 * T + even * T
    own_b = 2 * T + odd * T

    def aligned(value, step=None):
        return pl.multiple_of(value, T if step is None else step)

    def box(f, row, col, rows=T, cols=T):
        return ext.at[f, pl.ds(aligned(row), rows), pl.ds(aligned(col), cols)]

    def remote(src, dst, f, index, to):
        return pltpu.make_async_remote_copy(
            src_ref=src,
            dst_ref=dst,
            send_sem=send_sem.at[f, index],
            recv_sem=recv_sem.at[f, index],
            device_id=to,
            device_id_type=MESH,
        )

    def order(s):
        return lax.rem(3 * (s // 2), 4), lax.rem(s, 2)

    def rung_copy(f, s):
        q, heavy = order(s)
        half = odd * (1 - heavy) + even * heavy
        there = odd * (5 * T - heavy * T) + even * heavy * T
        return remote(
            box(f, 2 * T + half * T, 2 * T + q * T),
            box(f, there, 2 * T + q * T),
            f,
            s,
            (partner, c),
        )

    def arrived_row(heavy):
        return odd * heavy * T + even * (5 * T - heavy * T)

    def rail_copy(f, s):
        q, heavy = order(s)
        there = odd * (4 * T + heavy * T) + even * (T - heavy * T)
        return remote(
            box(f, arrived_row(heavy), 2 * T + q * T),
            box(f, there, 2 * T + q * T),
            f,
            STEPS + s,
            (fwd_row, c),
        )

    def side_index(side, message):
        return 2 * STEPS + 6 * side + message

    def there_col(side, far):
        return (6 * T + far * T) if side == 0 else (T - far * T)

    def here_col(side, far):
        return (2 * T + far * T) if side == 0 else (5 * T - far * T)

    def tile_copy(f, side, far, half, row, to):
        return remote(
            box(f, row, here_col(side, far)),
            box(f, 2 * T + half * T, there_col(side, far)),
            f,
            side_index(side, 2 * far + half),
            to,
        )

    def corner_copy(f, side, down, row, to):
        return remote(
            box(f, row, here_col(side, 0)),
            box(f, T + 3 * T * down, there_col(side, 0)),
            f,
            side_index(side, 4 + down),
            to,
        )

    def own_columns(f):
        for side, (col, edge) in enumerate(sides):
            @pl.when(jnp.logical_not(edge))
            def _():
                for far in range(2):
                    for half in range(2):
                        tile_copy(f, side, far, half, 2 * T + half * T, (r, col)).start()

            @pl.when(edge)
            def _():
                corner_copy(f, side, odd, 2 * T + even * T, (partner, col)).start()

                @pl.when(has_b)
                def _():
                    corner_copy(f, side, even, 2 * T + odd * T, (other, col)).start()

    def pass_tile(f, s):
        k = s // 2
        q = (3 * k) % 4
        heavy = s % 2
        side = 0 if q < 2 else 1
        far = 1 if q in (1, 2) else 0
        col, edge = sides[side]

        @pl.when(edge)
        def _():
            half = odd * heavy + even * (1 - heavy)
            tile_copy(f, side, far, half, arrived_row(heavy), (partner, col)).start()

    def pass_corners(f, side):
        col, edge = sides[side]

        @pl.when(jnp.logical_not(edge))
        def _():
            corner_copy(f, side, even, a_heavy, (r, col)).start()

            @pl.when(has_b)
            def _():
                corner_copy(f, side, odd, b_heavy, (r, col)).start()

    def wait_tile(f, side, far):
        for half in range(2):
            tile_copy(f, 1 - side, far, half, 2 * T, (r, c)).wait_recv()

    def wait_corners(f, side):
        corner_copy(f, 1 - side, even, 2 * T, (r, c)).wait_recv()

        @pl.when(has_b)
        def _():
            corner_copy(f, 1 - side, odd, 2 * T, (r, c)).wait_recv()

    def rate(f, src, row, col, coef_row, col_bands):
        wide = src[pl.ds(row, CHUNK), pl.ds(col - LANES, T + 2 * LANES)]
        tall = src[pl.ds(row - 8, CHUNK + 16), pl.ds(col, T)]

        def rows_of(k):
            band = row_coef[f, k, pl.ds(coef_row, CHUNK), :]
            return jnp.concatenate([band] * (T // LANES), axis=1)

        total = tall[8 : 8 + CHUNK] * (rows_of(0) + col_bands[0])
        for k, offset in enumerate(offsets):
            if k == 0:
                continue
            if abs(offset) < 8:
                by_row = pltpu.roll(tall, (-offset) % (CHUNK + 16), 0)[8 : 8 + CHUNK]
                by_col = pltpu.roll(wide, (-offset) % (T + 2 * LANES), 1)[:, LANES : LANES + T]
            else:
                by_row = src[pl.ds(row + offset, CHUNK), pl.ds(col, T)]
                by_col = src[pl.ds(row, CHUNK), pl.ds(col + offset, T)]
            total = total + rows_of(k) * by_row + col_bands[k] * by_col
        return total

    def bands_at(f, b):
        block = col_tab[pl.ds(aligned(f * 8, 8), 8), pl.ds(aligned((b + 1) * T), T)]
        return [jnp.broadcast_to(block[k : k + 1], (CHUNK, T)) for k in range(7)]

    def add_source(f, dst, row, col, coef_row, b, scale):
        tiles = n_cols * 4
        shift = lax.rem(4 * c + b - 2 * r - (coef_row // T - 1) + 2 * tiles + 1, tiles)

        @pl.when(jnp.logical_and(f == 0, shift <= 2))
        def _():
            def body(i, carry):
                values = row_tab[pl.ds(pl.multiple_of(coef_row + i * 8, 8), 8), :]
                here = lax.broadcasted_iota(jnp.int32, (8, T), 1) - lax.broadcasted_iota(
                    jnp.int32, (8, T), 0
                )
                here = here + (shift - 1) * T - i * 8
                at = pl.ds(pl.multiple_of(row + i * 8, 8), 8)
                total = dst[at, pl.ds(col, T)]
                for k, offset in enumerate(offsets):
                    feed = jnp.broadcast_to(values[:, 14 + k : 15 + k], (8, T))
                    total = total + jnp.where(here == offset, scale * feed, 0.0)
                dst[at, pl.ds(col, T)] = total
                return carry

            lax.fori_loop(0, T // 8, body, 0)

    def mid_tile(f, row, b):
        row = aligned(row)
        col = (b + 2) * T
        col_bands = bands_at(f, b)
        field = ext.at[f]

        def body(i, carry):
            at = pl.multiple_of(row + i * CHUNK, CHUNK)
            total = rate(f, field, at, col, pl.multiple_of(at - T, CHUNK), col_bands)
            total = total + field[pl.ds(at, CHUNK), pl.ds(col, T)]
            mid[pl.ds(pl.multiple_of(at - T, CHUNK), CHUNK), pl.ds(col - T, T)] = total
            return carry

        lax.fori_loop(0, T // CHUNK, body, 0)
        add_source(f, mid, aligned(row - T), col - T, aligned(row - T), b, 1.0)

    def own_mid(f, b):
        mid_tile(f, 2 * T, b)
        mid_tile(f, 3 * T, b)

    def mid_a(f, b):
        mid_tile(f, a_heavy, b)

    def mid_b(f, b):
        @pl.when(has_b)
        def _():
            mid_tile(f, b_heavy, b)

    def store_copy(k, half, b):
        out = (g_out, c_out)[k]
        rows, cols = pl.ds(aligned(half * T), T), pl.ds(b * T, T)
        return pltpu.make_async_copy(fin.at[k, rows, cols], out.at[rows, cols], store_sem.at[k, half * 4 + b])

    def out_tile(f, half, b):
        col_bands = bands_at(f, b)
        col = (b + 1) * T
        field = ext.at[f]
        done = fin.at[f]
        base = aligned(half * T)

        def body(i, carry):
            at = pl.multiple_of(base + i * CHUNK, CHUNK)
            inner = pl.multiple_of(at + T, CHUNK)
            total = rate(f, mid, inner, col, inner, col_bands)
            total = field[pl.ds(pl.multiple_of(at + 2 * T, CHUNK), CHUNK), pl.ds(col + T, T)] + 2.0 * total
            done[pl.ds(at, CHUNK), pl.ds(b * T, T)] = total
            return carry

        lax.fori_loop(0, T // CHUNK, body, 0)
        add_source(f, done, base, b * T, aligned(base + T), b, 2.0)
        for k in range(2):
            @pl.when(f == k)
            def _():
                store_copy(k, half, b).start()

    def out_pair(f, b):
        out_tile(f, 0, b)
        out_tile(f, 1, b)

    half_a = even
    half_b = odd

    def finish(f):
        wait_tile(f, 1, 1)
        own_mid(f, 4)
        out_pair(f, 3)

        @pl.when(has_b)
        def _():
            rail_copy(f, STEPS - 1).wait_recv()

        mid_b(f, 1)
        out_tile(f, half_b, 1)

    def tasks(f, s):
        if s == 1:
            pass_corners(f, 0)
        if s == 3:
            pass_corners(f, 1)
            wait_tile(f, 1, 0)
            own_mid(f, 3)
        if s == 5:
            wait_corners(f, 1)
            wait_tile(f, 0, 0)
            own_mid(f, 0)
            own_mid(f, 2)
            mid_a(f, 3)
            mid_b(f, 3)
        if s == 7:
            wait_corners(f, 0)
            wait_tile(f, 0, 1)
            own_mid(f, 1)
            own_mid(f, -1)
            for b in (0, 1, 2):
                mid_a(f, b)
            for b in (0, 2):
                mid_b(f, b)
            out_pair(f, 0)
            out_pair(f, 2)
            out_tile(f, half_a, 1)

    loads = [
        pltpu.make_async_copy(src, ext.at[k, pl.ds(2 * T, 2 * T), pl.ds(2 * T, 4 * T)], load_sem.at[k])
        for k, src in enumerate((g_hbm, c_hbm))
    ]
    for load in loads:
        load.start()

    barrier = pltpu.get_barrier_semaphore()

    def greet(row, col):
        pl.semaphore_signal(barrier, inc=1, device_id=(row, col), device_id_type=MESH)

    greet(partner, c)
    both = has_b.astype(jnp.int32)
    pl.when(has_fwd)(lambda: greet(fwd_row, c))
    pl.when(has_b)(lambda: greet(src_row, c))
    for col, edge in sides:
        pl.when(jnp.logical_not(edge))(lambda: greet(r, col))
        pl.when(edge)(lambda: greet(partner, col))
        pl.when(jnp.logical_and(edge, has_b))(lambda: greet(other, col))
    edges = left_edge.astype(jnp.int32) + right_edge.astype(jnp.int32)
    peers = 3 + has_fwd.astype(jnp.int32) + both + edges * both

    @pl.when(jnp.logical_not(has_b))
    def _():
        for k in range(2):
            ext[k, pl.ds(aligned(b_heavy), T), pl.ds(T, 6 * T)] = jnp.zeros((T, 6 * T), jnp.float32)
        mid[pl.ds(aligned(b_mid), T), :] = jnp.zeros((T, 6 * T), jnp.float32)

    pl.semaphore_wait(barrier, peers)
    loads[0].wait()
    for s in range(AHEAD):
        rung_copy(0, s).start()
    own_columns(0)
    loads[1].wait()

    def spread(i, carry):
        at = pl.ds(pl.multiple_of(i * 8, 8), 8)
        values = row_tab[at, :]
        for k in range(14):
            row_coef[k // 7, k % 7, at, :] = jnp.broadcast_to(values[:, k : k + 1], (8, LANES))
        return carry

    lax.fori_loop(0, 4 * T // 8, spread, 0)

    def field_steps(f, carry):
        for s in range(STEPS):
            rung_copy(f, s).wait_recv()
            pl.when(has_fwd)(lambda: rail_copy(f, s).start())
            pass_tile(f, s)
            if s + AHEAD < STEPS:
                rung_copy(f, s + AHEAD).start()
            else:
                pl.when(f == 0)(lambda: rung_copy(1, s + AHEAD - STEPS).start())
            if s == 4:
                pl.when(f == 0)(lambda: own_columns(1))
            if s == 0:
                pl.when(f == 1)(lambda: finish(0))
            else:
                pl.when(has_b)(lambda: rail_copy(f, s - 1).wait_recv())
            tasks(f, s)
        return carry

    lax.fori_loop(0, 2, field_steps, 0)
    finish(1)

    def drain(f, carry):
        for s in range(STEPS):
            rung_copy(f, s).wait_send()
            pl.when(has_fwd)(lambda: rail_copy(f, s).wait_send())
        for side in range(2):
            for far in range(2):
                for half in range(2):
                    tile_copy(f, side, far, half, 2 * T, (r, c)).wait_send()
            _, edge = sides[side]
            first = even + edge.astype(jnp.int32) * (odd - even)
            corner_copy(f, side, first, 2 * T, (r, c)).wait_send()
            second = 1 - first
            pl.when(has_b)(lambda: corner_copy(f, side, second, 2 * T, (r, c)).wait_send())
        return carry

    lax.fori_loop(0, 2, drain, 0)
    for half in range(2):
        for b in range(4):
            for k in range(2):
                store_copy(k, half, b).wait()


def shards(tile, n_rows, n_cols, group, g_start, cotangent, damping, hopping, bonds, source):
    T = tile
    modes = damping.shape[0]
    rows_dev, cols_dev = g_start.shape
    offsets = band_offsets(T // 2)
    row_first = lax.axis_index("row") * rows_dev
    col_first = lax.axis_index("col") * cols_dev
    coef = jnp.concatenate([-damping[None, :], hopping], axis=0) * bonds.astype(jnp.float32)
    both = (0.5 * DT) * jnp.concatenate([coef, source], axis=0)
    wrapped = jnp.concatenate([both[:, modes - 2 * T :], both, both[:, : 6 * T]], axis=1)
    near_rows = lax.dynamic_slice_in_dim(wrapped, row_first, 6 * T, 1)
    near_cols = lax.dynamic_slice_in_dim(wrapped, col_first, 8 * T, 1)

    def pick(window, count):
        forward = window[:7, T : T + count]
        adjoint = jnp.stack(
            [window[MIRROR[k], T + o : T + o + count] for k, o in enumerate(offsets)]
        )
        return forward, adjoint

    row_f, row_a = pick(near_rows, 4 * T)
    col_f, col_a = pick(near_cols, 6 * T)
    row_tab = jnp.concatenate([row_f, row_a, near_rows[7:, T : 5 * T]], axis=0)
    row_tab = jnp.pad(row_tab, ((0, LANES - 21), (0, 0))).T
    blank = jnp.zeros((1, 6 * T), jnp.float32)
    col_tab = jnp.concatenate([col_f, blank, col_a, blank], axis=0)

    block = jax.ShapeDtypeStruct((rows_dev, cols_dev), jnp.float32)
    sems = 2 * STEPS + 12
    return pl.pallas_call(
        functools.partial(kernel, T, n_rows, n_cols, group),
        out_shape=(block, block),
        in_specs=[
            pl.BlockSpec(memory_space=pl.ANY),
            pl.BlockSpec(memory_space=pl.ANY),
            pl.BlockSpec(memory_space=pltpu.VMEM),
            pl.BlockSpec(memory_space=pltpu.VMEM),
        ],
        out_specs=(pl.BlockSpec(memory_space=pl.ANY), pl.BlockSpec(memory_space=pl.ANY)),
        scratch_shapes=[
            pltpu.VMEM((2, 6 * T, 8 * T), jnp.float32),
            pltpu.VMEM((4 * T, 6 * T), jnp.float32),
            pltpu.VMEM((2, 2 * T, 4 * T), jnp.float32),
            pltpu.VMEM((2, 7, 4 * T, LANES), jnp.float32),
            pltpu.SemaphoreType.DMA((2,)),
            pltpu.SemaphoreType.DMA((2, 8)),
            pltpu.SemaphoreType.DMA((2, sems)),
            pltpu.SemaphoreType.DMA((2, sems)),
        ],
        compiler_params=pltpu.CompilerParams(
            collective_id=0, has_side_effects=True, vmem_limit_bytes=56 * 2**20
        ),
    )(g_start, cotangent, row_tab, col_tab)


def build(mesh, tile):
    n_rows = mesh.shape["row"]
    n_cols = mesh.shape["col"]
    return jax.shard_map(
        functools.partial(shards, tile, n_rows, n_cols, n_cols // 2),
        mesh=mesh,
        in_specs=(P("row", "col"), P("row", "col"), P(), P(), P(), P()),
        out_specs=(P("row", "col"), P("row", "col")),
        check_vma=False,
    )


def solution(mesh):
    return build(mesh, 2 * LX)
```

```python
import functools

import jax
import jax.numpy as jnp
from jax import lax
from jax.experimental import pallas as pl
from jax.experimental.pallas import tpu as pltpu
from jax.sharding import PartitionSpec as P

LX = 128
DT = 0.1
MESH = pl.DeviceIdType.MESH
STEPS = 8
AHEAD = 3
CHUNK = 32
LANES = 128


def band_offsets(side):
    return (0, 1, -1, 2, -2, 2 * side, -2 * side)


MIRROR = (0, 2, 1, 4, 3, 6, 5)


def kernel(
    tile,
    n_rows,
    n_cols,
    group,
    g_hbm,
    c_hbm,
    damping,
    hopping,
    bonds,
    source,
    g_out,
    c_out,
    ext,
    mid,
    fin,
    row_coef,
    col_tab,
    row_tab,
    win_damping,
    win_hopping,
    win_bonds,
    win_source,
    win_coef,
    load_sem,
    win_sem,
    store_sem,
    send_sem,
    recv_sem,
):
    T = tile
    offsets = band_offsets(T // 2)
    modes = 4 * T * n_cols
    r = lax.axis_index("row")
    c = lax.axis_index("col")
    odd = lax.rem(r, 2)
    even = 1 - odd
    partner = r + 1 - 2 * odd
    other = r - 1 + 2 * odd
    has_b = jnp.logical_and(other >= 0, other < n_rows)
    fwd_row = r + 2 - 4 * odd
    has_fwd = jnp.logical_and(fwd_row >= 0, fwd_row < n_rows)
    src_row = r - 2 + 4 * odd
    left = lax.rem(c + n_cols - 1, n_cols)
    right = lax.rem(c + 1, n_cols)
    left_edge = lax.rem(c, group) == 0
    right_edge = lax.rem(c, group) == group - 1
    sides = ((left, left_edge), (right, right_edge))

    def row_at(p):
        return T * (odd * (4 - p) + even * (1 + p))

    a_heavy = row_at(3)
    b_heavy = row_at(0)
    half_a = even
    half_b = odd

    def aligned(value, step=None):
        return pl.multiple_of(value, T if step is None else step)

    def box(f, row, col, rows=T, cols=T):
        return ext.at[f, pl.ds(aligned(row), rows), pl.ds(aligned(col), cols)]

    def remote(src, dst, f, index, to):
        return pltpu.make_async_remote_copy(
            src_ref=src,
            dst_ref=dst,
            send_sem=send_sem.at[f, index],
            recv_sem=recv_sem.at[f, index],
            device_id=to,
            device_id_type=MESH,
        )

    def order(s):
        return lax.rem(3 * lax.rem(s, 4), 4), s // 4

    def rung_copy(f, s):
        q, heavy = order(s)
        half = odd * (1 - heavy) + even * heavy
        there = odd * (5 * T - heavy * T) + even * heavy * T
        return remote(
            box(f, 2 * T + half * T, 2 * T + q * T),
            box(f, there, 2 * T + q * T),
            f,
            s,
            (partner, c),
        )

    def arrived_row(heavy):
        return odd * heavy * T + even * (5 * T - heavy * T)

    def rail_copy(f, s):
        q, heavy = order(s)
        there = odd * (4 * T + heavy * T) + even * (T - heavy * T)
        return remote(
            box(f, arrived_row(heavy), 2 * T + q * T),
            box(f, there, 2 * T + q * T),
            f,
            STEPS + s,
            (fwd_row, c),
        )

    def side_index(side, message):
        return 2 * STEPS + 6 * side + message

    def there_col(side, far):
        return (6 * T + far * T) if side == 0 else (T - far * T)

    def here_col(side, far):
        return (2 * T + far * T) if side == 0 else (5 * T - far * T)

    def tile_copy(f, side, far, half, row, to):
        return remote(
            box(f, row, here_col(side, far)),
            box(f, 2 * T + half * T, there_col(side, far)),
            f,
            side_index(side, 2 * far + half),
            to,
        )

    def corner_copy(f, side, down, row, to):
        return remote(
            box(f, row, here_col(side, 0)),
            box(f, T + 3 * T * down, there_col(side, 0)),
            f,
            side_index(side, 4 + down),
            to,
        )

    def own_columns(f):
        for side, (col, edge) in enumerate(sides):
            @pl.when(jnp.logical_not(edge))
            def _():
                for far in range(2):
                    for half in range(2):
                        tile_copy(f, side, far, half, 2 * T + half * T, (r, col)).start()

            @pl.when(edge)
            def _():
                corner_copy(f, side, odd, 2 * T + even * T, (partner, col)).start()

                @pl.when(has_b)
                def _():
                    corner_copy(f, side, even, 2 * T + odd * T, (other, col)).start()

    def pass_tile(f, s):
        q = (3 * (s % 4)) % 4
        heavy = s // 4
        side = 0 if q < 2 else 1
        far = 1 if q in (1, 2) else 0
        col, edge = sides[side]

        @pl.when(edge)
        def _():
            half = odd * heavy + even * (1 - heavy)
            tile_copy(f, side, far, half, arrived_row(heavy), (partner, col)).start()

    def pass_a_corner(f, side):
        col, edge = sides[side]

        @pl.when(jnp.logical_not(edge))
        def _():
            corner_copy(f, side, even, a_heavy, (r, col)).start()

    def pass_b_corner(f, side):
        col, edge = sides[side]

        @pl.when(jnp.logical_and(has_b, jnp.logical_not(edge)))
        def _():
            corner_copy(f, side, odd, b_heavy, (r, col)).start()

    def wait_tile(f, side, far, half):
        tile_copy(f, 1 - side, far, half, 2 * T, (r, c)).wait_recv()

    def wait_a_corner(f, side):
        corner_copy(f, 1 - side, even, 2 * T, (r, c)).wait_recv()

    def wait_b_corner(f, side):
        @pl.when(has_b)
        def _():
            corner_copy(f, 1 - side, odd, 2 * T, (r, c)).wait_recv()

    def spread_lanes(band):
        return jnp.concatenate([band] * (T // LANES), axis=1)

    def rate(f, src, row, col, coef_row, col_bands):
        wide = src[pl.ds(row, CHUNK), pl.ds(aligned(col - LANES, LANES), T + 2 * LANES)]
        tall = src[pl.ds(aligned(row - 8, 8), CHUNK + 16), pl.ds(col, T)]

        def rows_of(k):
            return spread_lanes(row_coef[7 * f + k, pl.ds(coef_row, CHUNK), :])

        total = tall[8 : 8 + CHUNK] * (rows_of(0) + col_bands[0])
        for k, offset in enumerate(offsets):
            if k == 0:
                continue
            if abs(offset) < 8:
                by_row = pltpu.roll(tall, (-offset) % (CHUNK + 16), 0)[8 : 8 + CHUNK]
                by_col = pltpu.roll(wide, (-offset) % (T + 2 * LANES), 1)[:, LANES : LANES + T]
            else:
                by_row = src[pl.ds(aligned(row + offset, CHUNK), CHUNK), pl.ds(col, T)]
                by_col = src[pl.ds(row, CHUNK), pl.ds(aligned(col + offset), T)]
            total = total + rows_of(k) * by_row + col_bands[k] * by_col
        return total

    def bands_at(f, b):
        block = col_tab[pl.ds(aligned(f * 8, 8), 8), pl.ds(aligned((b + 1) * T), T)]
        return [jnp.broadcast_to(block[k : k + 1], (CHUNK, T)) for k in range(7)]

    def add_source(f, dst, row, col, coef_row, b, scale):
        tiles = n_cols * 4
        shift = lax.rem(4 * c + b - 2 * r - (coef_row // T - 1) + 2 * tiles + 1, tiles)

        @pl.when(jnp.logical_and(f == 0, shift <= 2))
        def _():
            def body(i, carry):
                here = lax.broadcasted_iota(jnp.int32, (CHUNK, T), 1) - lax.broadcasted_iota(
                    jnp.int32, (CHUNK, T), 0
                )
                here = here + (shift - 1) * T - i * CHUNK
                at = pl.ds(aligned(row + i * CHUNK, CHUNK), CHUNK)
                total = dst[at, pl.ds(col, T)]
                for k, offset in enumerate(offsets):
                    feed = row_coef[14 + k, pl.ds(aligned(coef_row + i * CHUNK, CHUNK), CHUNK), :]
                    total = total + jnp.where(here == offset, spread_lanes(scale * feed), 0.0)
                dst[at, pl.ds(col, T)] = total
                return carry

            lax.fori_loop(0, T // CHUNK, body, 0)

    def mid_tile(f, row, b):
        row = aligned(row)
        col = aligned((b + 2) * T)
        inner = aligned((b + 1) * T)
        col_bands = bands_at(f, b)
        field = ext.at[f]

        def body(i, carry):
            at = aligned(row + i * CHUNK, CHUNK)
            low = aligned(row - T + i * CHUNK, CHUNK)
            total = rate(f, field, at, col, low, col_bands)
            total = total + field[pl.ds(at, CHUNK), pl.ds(col, T)]
            mid[pl.ds(low, CHUNK), pl.ds(inner, T)] = total
            return carry

        lax.fori_loop(0, T // CHUNK, body, 0, unroll=True)
        add_source(f, mid, aligned(row - T), inner, aligned(row - T), b, 1.0)

    def mids(f, jobs):
        packed = sum((8 * p + b + 1) << (5 * i) for i, (p, b) in enumerate(jobs))

        def body(_, rest):
            p = lax.rem(rest, 32) // 8
            b = lax.rem(rest, 8) - 1

            @pl.when(jnp.logical_or(p > 0, has_b))
            def _():
                mid_tile(f, row_at(p), b)

            return rest // 32

        lax.fori_loop(0, len(jobs), body, jnp.int32(packed))

    def store_copy(k, half, b):
        out = (g_out, c_out)[k]
        rows, cols = pl.ds(aligned(half * T), T), pl.ds(aligned(b * T), T)
        return pltpu.make_async_copy(fin.at[k, rows, cols], out.at[rows, cols], store_sem.at[k, half * 4 + b])

    def out_tile(f, half, b):
        col_bands = bands_at(f, b)
        col = aligned((b + 1) * T)
        outer = aligned((b + 2) * T)
        own = aligned(b * T)
        field = ext.at[f]
        done = fin.at[f]
        base = aligned(half * T)

        def body(i, carry):
            at = aligned(base + i * CHUNK, CHUNK)
            inner = aligned(base + T + i * CHUNK, CHUNK)
            total = rate(f, mid, inner, col, inner, col_bands)
            total = field[pl.ds(aligned(base + 2 * T + i * CHUNK, CHUNK), CHUNK), pl.ds(outer, T)] + 2.0 * total
            done[pl.ds(at, CHUNK), pl.ds(own, T)] = total
            return carry

        lax.fori_loop(0, T // CHUNK, body, 0, unroll=True)
        add_source(f, done, base, own, aligned(base + T), b, 2.0)
        for k in range(2):
            @pl.when(f == k)
            def _():
                store_copy(k, half, b).start()

    def outs(f, jobs):
        packed = sum((4 * e + b) << (3 * i) for i, (e, b) in enumerate(jobs))

        def body(_, rest):
            e = lax.rem(rest, 8) // 4
            b = lax.rem(rest, 4)
            out_tile(f, (1 - e) * half_a + e * half_b, b)
            return rest // 8

        lax.fori_loop(0, len(jobs), body, jnp.int32(packed))

    def finish(f):
        wait_tile(f, 1, 1, half_a)

        @pl.when(has_b)
        def _():
            rail_copy(f, STEPS - 1).wait_recv()

        mids(f, ((2, 4), (0, 1)))
        outs(f, ((0, 3), (1, 1)))

    def tasks(f, s):
        if s == 1:
            pass_b_corner(f, 0)
        if s == 2:
            pass_b_corner(f, 1)
            wait_tile(f, 0, 0, half_b)
            wait_tile(f, 1, 0, half_b)
            mids(f, ((1, 0), (1, 3)))
        if s == 4:
            pass_a_corner(f, 0)
            mids(f, ((1, 2), (1, 1)))
        if s == 5:
            pass_a_corner(f, 1)
            wait_b_corner(f, 0)
            wait_b_corner(f, 1)
            wait_tile(f, 1, 0, half_a)
            wait_tile(f, 1, 1, half_b)
            mids(f, ((0, 0), (2, 3), (1, 4)))
        if s == 6:
            wait_tile(f, 0, 0, half_a)
            wait_tile(f, 0, 1, half_b)
            wait_a_corner(f, 1)
            mids(f, ((1, -1), (2, 0), (2, 2), (0, 3), (3, 3)))
            outs(f, ((1, 0), (1, 3)))
        if s == 7:
            wait_a_corner(f, 0)
            wait_tile(f, 0, 1, half_a)
            mids(f, ((2, 1), (2, -1), (3, 0), (3, 1), (3, 2), (0, 2)))
            outs(f, ((0, 0), (0, 1), (0, 2), (1, 2)))

    row_first = r * 2 * T
    col_first = c * 4 * T
    spans = (
        (0, row_first + modes - 2 * T, 2 * T),
        (2 * T, row_first, 4 * T),
        (6 * T, col_first + modes - 2 * T, 2 * T),
        (8 * T, col_first, 4 * T),
        (12 * T, col_first + 4 * T, 2 * T),
    )
    arrays = (
        (damping, win_damping),
        (hopping, win_hopping),
        (bonds, win_bonds),
        (source, win_source),
    )

    def window_copies():
        for k, (src, dst) in enumerate(arrays):
            for i, (at, first, count) in enumerate(spans):
                start = aligned(lax.rem(first, modes), 2 * T)
                yield pltpu.make_async_copy(
                    src.at[:, pl.ds(start, count)], dst.at[:, pl.ds(at, count)], win_sem.at[k, i]
                )

    loads = [
        pltpu.make_async_copy(src, ext.at[k, pl.ds(2 * T, 2 * T), pl.ds(2 * T, 4 * T)], load_sem.at[k])
        for k, src in enumerate((g_hbm, c_hbm))
    ]
    barrier = pltpu.get_barrier_semaphore()

    def greet(row, col):
        pl.semaphore_signal(barrier, inc=1, device_id=(row, col), device_id_type=MESH)

    greet(partner, c)
    both = has_b.astype(jnp.int32)
    pl.when(has_fwd)(lambda: greet(fwd_row, c))
    pl.when(has_b)(lambda: greet(src_row, c))
    for col, edge in sides:
        pl.when(jnp.logical_not(edge))(lambda: greet(r, col))
        pl.when(edge)(lambda: greet(partner, col))
        pl.when(jnp.logical_and(edge, has_b))(lambda: greet(other, col))
    edges = left_edge.astype(jnp.int32) + right_edge.astype(jnp.int32)
    peers = 3 + has_fwd.astype(jnp.int32) + both + edges * both

    for load in loads:
        load.start()
    for copy in window_copies():
        copy.start()

    loads[0].wait()
    pl.semaphore_wait(barrier, peers)
    for s in range(AHEAD):
        rung_copy(0, s).start()
    own_columns(0)

    @pl.when(jnp.logical_not(has_b))
    def _():
        for k in range(2):
            ext[k, pl.ds(aligned(b_heavy), T), pl.ds(T, 6 * T)] = jnp.zeros((T, 6 * T), jnp.float32)
        mid[pl.ds(aligned(b_heavy - T), T), :] = jnp.zeros((T, 6 * T), jnp.float32)

    for copy in window_copies():
        copy.wait()
    half_step = 0.5 * DT
    present = win_bonds[...].astype(jnp.float32)
    win_coef[0:1, :] = -half_step * win_damping[...] * present[0:1]
    win_coef[1:7, :] = half_step * win_hopping[...] * present[1:7]
    win_coef[7:8, :] = jnp.zeros((1, 14 * T), jnp.float32)

    def adjoint(first, count):
        window = win_coef[:, first : first + count + 2 * T]
        rows = []
        for k, offset in enumerate(offsets):
            band = window[MIRROR[k] : MIRROR[k] + 1]
            rows.append(pltpu.roll(band, (-offset) % (count + 2 * T), 1)[:, T : T + count])
        return rows

    row_tab[...] = jnp.zeros_like(row_tab)
    row_tab[0:8, :] = win_coef[:, T : 5 * T]
    for k, band in enumerate(adjoint(0, 4 * T)):
        row_tab[7 + k : 8 + k, :] = band
    row_tab[14:21, :] = half_step * win_source[:, T : 5 * T]
    col_tab[0:8, :] = win_coef[:, 7 * T : 13 * T]
    for k, band in enumerate(adjoint(6 * T, 6 * T)):
        col_tab[8 + k : 9 + k, :] = band
    for i in range(4 * T // LANES):
        block = row_tab[:, i * LANES : (i + 1) * LANES].T
        for k in range(21):
            row_coef[k, i * LANES : (i + 1) * LANES, :] = jnp.broadcast_to(block[:, k : k + 1], (LANES, LANES))

    loads[1].wait()

    def field_steps(f, carry):
        for s in range(STEPS):
            rung_copy(f, s).wait_recv()
            pl.when(has_fwd)(lambda: rail_copy(f, s).start())
            pass_tile(f, s)
            if s + AHEAD < STEPS:
                rung_copy(f, s + AHEAD).start()
            else:
                pl.when(f == 0)(lambda: rung_copy(1, s + AHEAD - STEPS).start())
            if s == 3:
                pl.when(f == 0)(lambda: own_columns(1))
            if s == 0:
                pl.when(f == 1)(lambda: finish(0))
            else:
                pl.when(has_b)(lambda: rail_copy(f, s - 1).wait_recv())
            tasks(f, s)
        return carry

    lax.fori_loop(0, 2, field_steps, 0)
    finish(1)

    def drain(f, carry):
        for s in range(STEPS):
            rung_copy(f, s).wait_send()
            pl.when(has_fwd)(lambda: rail_copy(f, s).wait_send())
        for side in range(2):
            for far in range(2):
                for half in range(2):
                    tile_copy(f, side, far, half, 2 * T, (r, c)).wait_send()
            _, edge = sides[side]
            first = even + edge.astype(jnp.int32) * (odd - even)
            corner_copy(f, side, first, 2 * T, (r, c)).wait_send()
            pl.when(has_b)(lambda: corner_copy(f, side, 1 - first, 2 * T, (r, c)).wait_send())
        return carry

    lax.fori_loop(0, 2, drain, 0)
    for half in range(2):
        for b in range(4):
            for k in range(2):
                store_copy(k, half, b).wait()


def shards(tile, n_rows, n_cols, group, g_start, cotangent, damping, hopping, bonds, source):
    T = tile
    block = jax.ShapeDtypeStruct(g_start.shape, jnp.float32)
    sems = 2 * STEPS + 12
    anywhere = pl.BlockSpec(memory_space=pl.ANY)
    return pl.pallas_call(
        functools.partial(kernel, T, n_rows, n_cols, group),
        out_shape=(block, block),
        in_specs=[anywhere] * 6,
        out_specs=(anywhere, anywhere),
        scratch_shapes=[
            pltpu.VMEM((2, 6 * T, 8 * T), jnp.float32),
            pltpu.VMEM((4 * T, 6 * T), jnp.float32),
            pltpu.VMEM((2, 2 * T, 4 * T), jnp.float32),
            pltpu.VMEM((21, 4 * T, LANES), jnp.float32),
            pltpu.VMEM((16, 6 * T), jnp.float32),
            pltpu.VMEM((LANES, 4 * T), jnp.float32),
            pltpu.VMEM((1, 14 * T), jnp.float32),
            pltpu.VMEM((6, 14 * T), jnp.float32),
            pltpu.VMEM((7, 14 * T), jnp.int32),
            pltpu.VMEM((7, 14 * T), jnp.float32),
            pltpu.VMEM((8, 14 * T), jnp.float32),
            pltpu.SemaphoreType.DMA((2,)),
            pltpu.SemaphoreType.DMA((4, 5)),
            pltpu.SemaphoreType.DMA((2, 8)),
            pltpu.SemaphoreType.DMA((2, sems)),
            pltpu.SemaphoreType.DMA((2, sems)),
        ],
        compiler_params=pltpu.CompilerParams(
            collective_id=0, has_side_effects=True, vmem_limit_bytes=56 * 2**20
        ),
    )(g_start, cotangent, damping.reshape(1, -1), hopping, bonds, source)


def build(mesh, tile):
    n_rows = mesh.shape["row"]
    n_cols = mesh.shape["col"]
    return jax.shard_map(
        functools.partial(shards, tile, n_rows, n_cols, n_cols // 2),
        mesh=mesh,
        in_specs=(P("row", "col"), P("row", "col"), P(), P(), P(), P()),
        out_specs=(P("row", "col"), P("row", "col")),
        check_vma=False,
    )


def solution(mesh):
    return build(mesh, 2 * LX)
```

```python
import functools

import jax
import jax.numpy as jnp
from jax import lax
from jax.experimental import pallas as pl
from jax.experimental.pallas import tpu as pltpu
from jax.sharding import PartitionSpec as P

LX = 128
DT = 0.1
MESH = pl.DeviceIdType.MESH
STEPS = 8
AHEAD = 3
PIECES = (1, 1, 1, 1, 1, 1, 2, 4)
EXTRA = sum(PIECES) - STEPS
CHUNK = 32
LANES = 128


def band_offsets(side):
    return (0, 1, -1, 2, -2, 2 * side, -2 * side)


MIRROR = (0, 2, 1, 4, 3, 6, 5)


def kernel(
    tile,
    n_rows,
    n_cols,
    group,
    g_hbm,
    c_hbm,
    damping,
    hopping,
    bonds,
    source,
    fin,
    ext,
    mid,
    row_coef,
    col_tab,
    row_tab,
    win_damping,
    win_hopping,
    win_bonds,
    win_source,
    win_coef,
    load_sem,
    win_sem,
    send_sem,
    recv_sem,
):
    T = tile
    offsets = band_offsets(T // 2)
    modes = 4 * T * n_cols
    r = lax.axis_index("row")
    c = lax.axis_index("col")
    odd = lax.rem(r, 2)
    even = 1 - odd
    partner = r + 1 - 2 * odd
    other = r - 1 + 2 * odd
    has_b = jnp.logical_and(other >= 0, other < n_rows)
    fwd_row = r + 2 - 4 * odd
    has_fwd = jnp.logical_and(fwd_row >= 0, fwd_row < n_rows)
    src_row = r - 2 + 4 * odd
    left = lax.rem(c + n_cols - 1, n_cols)
    right = lax.rem(c + 1, n_cols)
    left_edge = lax.rem(c, group) == 0
    right_edge = lax.rem(c, group) == group - 1
    sides = ((left, left_edge), (right, right_edge))

    def row_at(p):
        return T * (odd * (4 - p) + even * (1 + p))

    a_heavy = row_at(3)
    b_heavy = row_at(0)
    half_a = even
    half_b = odd

    def aligned(value, step=None):
        return pl.multiple_of(value, T if step is None else step)

    def box(f, row, col, rows=T):
        return ext.at[f, pl.ds(aligned(row, rows), rows), pl.ds(aligned(col), T)]

    def remote(src, dst, f, index, to):
        return pltpu.make_async_remote_copy(
            src_ref=src,
            dst_ref=dst,
            send_sem=send_sem.at[f, index],
            recv_sem=recv_sem.at[f, index],
            device_id=to,
            device_id_type=MESH,
        )

    def order(s):
        return (3 * (s % 4)) % 4, s // 4

    def piece_of(s, i):
        rows = T // PIECES[s]
        return rows, i * rows, sum(PIECES[:s]) + i

    def rung_copy(f, s, i, src=None):
        q, heavy = order(s)
        rows, first, index = piece_of(s, i)
        half = odd * (1 - heavy) + even * heavy
        there = odd * (5 * T - heavy * T) + even * heavy * T
        if src is None:
            src = box(f, 2 * T + half * T + first, 2 * T + q * T, rows)
        else:
            src = src.at[pl.ds(aligned(half * T + first, rows), rows), pl.ds(q * T, T)]
        return remote(src, box(f, there + first, 2 * T + q * T, rows), f, index, (partner, c))

    def arrived_row(heavy):
        return odd * heavy * T + even * (5 * T - heavy * T)

    def rail_copy(f, s, i):
        q, heavy = order(s)
        rows, first, index = piece_of(s, i)
        there = odd * (4 * T + heavy * T) + even * (T - heavy * T)
        return remote(
            box(f, arrived_row(heavy) + first, 2 * T + q * T, rows),
            box(f, there + first, 2 * T + q * T, rows),
            f,
            STEPS + EXTRA + index,
            (fwd_row, c),
        )

    def wait_rail(f, s):
        @pl.when(has_b)
        def _():
            for i in range(PIECES[s]):
                rail_copy(f, s, i).wait_recv()

    def side_index(side, message):
        return 2 * (STEPS + EXTRA) + 6 * side + message

    def there_col(side, far):
        return (6 * T + far * T) if side == 0 else (T - far * T)

    def here_col(side, far):
        return (2 * T + far * T) if side == 0 else (5 * T - far * T)

    def tile_copy(f, side, far, half, row, to, rows=T, first=0):
        return remote(
            box(f, row + first, here_col(side, far), rows),
            box(f, 2 * T + half * T + first, there_col(side, far), rows),
            f,
            side_index(side, 2 * far + half),
            to,
        )

    def corner_copy(f, side, down, row, to):
        return remote(
            box(f, row, here_col(side, 0)),
            box(f, T + 3 * T * down, there_col(side, 0)),
            f,
            side_index(side, 4 + down),
            to,
        )

    def own_columns(f):
        for side, (col, edge) in enumerate(sides):
            @pl.when(jnp.logical_not(edge))
            def _():
                for far in range(2):
                    for half in range(2):
                        tile_copy(f, side, far, half, 2 * T + half * T, (r, col)).start()

            @pl.when(edge)
            def _():
                corner_copy(f, side, odd, 2 * T + even * T, (partner, col)).start()

                @pl.when(has_b)
                def _():
                    corner_copy(f, side, even, 2 * T + odd * T, (other, col)).start()

    def pass_tile(f, s, i):
        rows, first, _ = piece_of(s, i)
        q = (3 * (s % 4)) % 4
        heavy = s // 4
        side = 0 if q < 2 else 1
        far = 1 if q in (1, 2) else 0
        col, edge = sides[side]

        @pl.when(edge)
        def _():
            half = odd * heavy + even * (1 - heavy)
            tile_copy(f, side, far, half, arrived_row(heavy), (partner, col), rows, first).start()

    def pass_a_corner(f, side):
        col, edge = sides[side]

        @pl.when(jnp.logical_not(edge))
        def _():
            corner_copy(f, side, even, a_heavy, (r, col)).start()

    def pass_b_corner(f, side):
        col, edge = sides[side]

        @pl.when(jnp.logical_and(has_b, jnp.logical_not(edge)))
        def _():
            corner_copy(f, side, odd, b_heavy, (r, col)).start()

    def wait_tile(f, side, far, half):
        tile_copy(f, 1 - side, far, half, 2 * T, (r, c)).wait_recv()

    def wait_a_corner(f, side):
        corner_copy(f, 1 - side, even, 2 * T, (r, c)).wait_recv()

    def wait_b_corner(f, side):
        @pl.when(has_b)
        def _():
            corner_copy(f, 1 - side, odd, 2 * T, (r, c)).wait_recv()

    def spread_lanes(band):
        return jnp.concatenate([band] * (T // LANES), axis=1)

    def rate(f, src, row, col, coef_row, col_bands):
        wide = src[pl.ds(row, CHUNK), pl.ds(aligned(col - LANES, LANES), T + 2 * LANES)]
        tall = src[pl.ds(aligned(row - 8, 8), CHUNK + 16), pl.ds(col, T)]

        def rows_of(k):
            return spread_lanes(row_coef[7 * f + k, pl.ds(coef_row, CHUNK), :])

        total = tall[8 : 8 + CHUNK] * (rows_of(0) + col_bands[0])
        for k, offset in enumerate(offsets):
            if k == 0:
                continue
            if abs(offset) < 8:
                by_row = pltpu.roll(tall, (-offset) % (CHUNK + 16), 0)[8 : 8 + CHUNK]
                by_col = pltpu.roll(wide, (-offset) % (T + 2 * LANES), 1)[:, LANES : LANES + T]
            else:
                by_row = src[pl.ds(aligned(row + offset, CHUNK), CHUNK), pl.ds(col, T)]
                by_col = src[pl.ds(row, CHUNK), pl.ds(aligned(col + offset), T)]
            total = total + rows_of(k) * by_row + col_bands[k] * by_col
        return total

    def bands_at(f, b):
        block = col_tab[pl.ds(aligned(f * 8, 8), 8), pl.ds(aligned((b + 1) * T), T)]
        return [jnp.broadcast_to(block[k : k + 1], (CHUNK, T)) for k in range(7)]

    def add_source(f, dst, row, col, coef_row, b, scale):
        tiles = n_cols * 4
        shift = lax.rem(4 * c + b - 2 * r - (coef_row // T - 1) + 2 * tiles + 1, tiles)

        @pl.when(jnp.logical_and(f == 0, shift <= 2))
        def _():
            def body(i, carry):
                here = lax.broadcasted_iota(jnp.int32, (CHUNK, T), 1) - lax.broadcasted_iota(
                    jnp.int32, (CHUNK, T), 0
                )
                here = here + (shift - 1) * T - i * CHUNK
                at = pl.ds(aligned(row + i * CHUNK, CHUNK), CHUNK)
                total = dst[at, pl.ds(col, T)]
                for k, offset in enumerate(offsets):
                    feed = row_coef[14 + k, pl.ds(aligned(coef_row + i * CHUNK, CHUNK), CHUNK), :]
                    total = total + jnp.where(here == offset, spread_lanes(scale * feed), 0.0)
                dst[at, pl.ds(col, T)] = total
                return carry

            lax.fori_loop(0, T // CHUNK, body, 0)

    def mid_tile(f, row, b):
        row = aligned(row)
        col = aligned((b + 2) * T)
        inner = aligned((b + 1) * T)
        col_bands = bands_at(f, b)
        field = ext.at[f]

        def body(i, carry):
            at = aligned(row + i * CHUNK, CHUNK)
            low = aligned(row - T + i * CHUNK, CHUNK)
            total = rate(f, field, at, col, low, col_bands)
            total = total + field[pl.ds(at, CHUNK), pl.ds(col, T)]
            mid[pl.ds(low, CHUNK), pl.ds(inner, T)] = total
            return carry

        lax.fori_loop(0, T // CHUNK, body, 0, unroll=True)
        add_source(f, mid, aligned(row - T), inner, aligned(row - T), b, 1.0)

    def mids(f, jobs):
        packed = sum((8 * p + b + 1) << (5 * i) for i, (p, b) in enumerate(jobs))

        def body(_, rest):
            p = lax.rem(rest, 32) // 8
            b = lax.rem(rest, 8) - 1

            @pl.when(jnp.logical_or(p > 0, has_b))
            def _():
                mid_tile(f, row_at(p), b)

            return rest // 32

        lax.fori_loop(0, len(jobs), body, jnp.int32(packed))

    def out_tile(f, half, b):
        col_bands = bands_at(f, b)
        col = aligned((b + 1) * T)
        outer = aligned((b + 2) * T)
        own = aligned(b * T)
        field = ext.at[f]
        done = fin.at[f]
        base = aligned(half * T)

        def body(i, carry):
            at = aligned(base + i * CHUNK, CHUNK)
            inner = aligned(base + T + i * CHUNK, CHUNK)
            total = rate(f, mid, inner, col, inner, col_bands)
            total = field[pl.ds(aligned(base + 2 * T + i * CHUNK, CHUNK), CHUNK), pl.ds(outer, T)] + 2.0 * total
            done[pl.ds(at, CHUNK), pl.ds(own, T)] = total
            return carry

        lax.fori_loop(0, T // CHUNK, body, 0, unroll=True)
        add_source(f, done, base, own, aligned(base + T), b, 2.0)

    def outs(f, jobs):
        packed = sum((4 * e + b) << (3 * i) for i, (e, b) in enumerate(jobs))

        def body(_, rest):
            e = lax.rem(rest, 8) // 4
            b = lax.rem(rest, 4)
            out_tile(f, (1 - e) * half_a + e * half_b, b)
            return rest // 8

        lax.fori_loop(0, len(jobs), body, jnp.int32(packed))

    def finish(f):
        wait_tile(f, 1, 1, half_a)
        wait_rail(f, 7)
        mids(f, ((2, 4), (0, 1)))
        outs(f, ((1, 1), (0, 3)))

    def tasks(f, s):
        if s == 1:
            wait_rail(f, 0)
            pass_b_corner(f, 0)
        if s == 2:
            wait_rail(f, 1)
            pass_b_corner(f, 1)
            wait_tile(f, 0, 0, half_b)
            wait_tile(f, 1, 0, half_b)
            mids(f, ((1, 0), (1, 3)))
        if s == 4:
            pass_a_corner(f, 0)
            wait_rail(f, 2)
            wait_rail(f, 3)
            mids(f, ((1, 2), (1, 1)))
        if s == 5:
            pass_a_corner(f, 1)
            wait_rail(f, 4)
            wait_b_corner(f, 0)
            wait_b_corner(f, 1)
            wait_tile(f, 1, 0, half_a)
            wait_tile(f, 1, 1, half_b)
            mids(f, ((0, 0), (2, 3), (1, 4)))
        if s == 6:
            wait_tile(f, 0, 0, half_a)
            wait_tile(f, 0, 1, half_b)
            wait_a_corner(f, 1)
            wait_rail(f, 5)
            mids(f, ((1, -1), (2, 0), (2, 2), (0, 3), (3, 3)))
            outs(f, ((1, 0), (1, 3)))
            wait_rail(f, 6)
            mids(f, ((0, 2),))
        if s == 7:
            wait_a_corner(f, 0)
            mids(f, ((2, 1), (3, 0), (3, 1), (3, 2)))
            outs(f, ((0, 1), (0, 2), (1, 2)))
            wait_tile(f, 0, 1, half_a)
            mids(f, ((2, -1),))
            outs(f, ((0, 0),))

    row_first = r * 2 * T
    col_first = c * 4 * T
    spans = (
        (0, row_first + modes - 2 * T, 2 * T),
        (2 * T, row_first, 4 * T),
        (6 * T, col_first + modes - 2 * T, 2 * T),
        (8 * T, col_first, 4 * T),
        (12 * T, col_first + 4 * T, 2 * T),
    )
    arrays = (
        (damping, win_damping),
        (hopping, win_hopping),
        (bonds, win_bonds),
        (source, win_source),
    )

    def window_copies():
        for k, (src, dst) in enumerate(arrays):
            for i, (at, first, count) in enumerate(spans):
                start = aligned(lax.rem(first, modes), 2 * T)
                yield pltpu.make_async_copy(
                    src.at[:, pl.ds(start, count)], dst.at[:, pl.ds(at, count)], win_sem.at[k, i]
                )

    loads = [
        pltpu.make_async_copy(src, ext.at[k, pl.ds(2 * T, 2 * T), pl.ds(2 * T, 4 * T)], load_sem.at[k])
        for k, src in enumerate((g_hbm, c_hbm))
    ]
    barrier = pltpu.get_barrier_semaphore()

    def greet(row, col):
        pl.semaphore_signal(barrier, inc=1, device_id=(row, col), device_id_type=MESH)

    greet(partner, c)
    both = has_b.astype(jnp.int32)
    pl.when(has_fwd)(lambda: greet(fwd_row, c))
    pl.when(has_b)(lambda: greet(src_row, c))
    for col, edge in sides:
        pl.when(jnp.logical_not(edge))(lambda: greet(r, col))
        pl.when(edge)(lambda: greet(partner, col))
        pl.when(jnp.logical_and(edge, has_b))(lambda: greet(other, col))
    edges = left_edge.astype(jnp.int32) + right_edge.astype(jnp.int32)
    peers = 3 + has_fwd.astype(jnp.int32) + both + edges * both

    for load in loads:
        load.start()
    for copy in window_copies():
        copy.start()

    pl.semaphore_wait(barrier, peers)
    for s in range(AHEAD):
        rung_copy(0, s, 0, g_hbm).start()
    loads[0].wait()
    own_columns(0)

    @pl.when(jnp.logical_not(has_b))
    def _():
        for k in range(2):
            ext[k, pl.ds(aligned(b_heavy), T), pl.ds(T, 6 * T)] = jnp.zeros((T, 6 * T), jnp.float32)
        mid[pl.ds(aligned(b_heavy - T), T), :] = jnp.zeros((T, 6 * T), jnp.float32)

    for copy in window_copies():
        copy.wait()
    half_step = 0.5 * DT
    present = win_bonds[...].astype(jnp.float32)
    win_coef[0:1, :] = -half_step * win_damping[...] * present[0:1]
    win_coef[1:7, :] = half_step * win_hopping[...] * present[1:7]
    win_coef[7:8, :] = jnp.zeros((1, 14 * T), jnp.float32)

    def adjoint(first, count):
        window = win_coef[:, first : first + count + 2 * T]
        rows = []
        for k, offset in enumerate(offsets):
            band = window[MIRROR[k] : MIRROR[k] + 1]
            rows.append(pltpu.roll(band, (-offset) % (count + 2 * T), 1)[:, T : T + count])
        return rows

    row_tab[...] = jnp.zeros_like(row_tab)
    row_tab[0:8, :] = win_coef[:, T : 5 * T]
    for k, band in enumerate(adjoint(0, 4 * T)):
        row_tab[7 + k : 8 + k, :] = band
    row_tab[14:21, :] = half_step * win_source[:, T : 5 * T]
    col_tab[0:8, :] = win_coef[:, 7 * T : 13 * T]
    for k, band in enumerate(adjoint(6 * T, 6 * T)):
        col_tab[8 + k : 9 + k, :] = band
    for i in range(4 * T // LANES):
        block = row_tab[:, i * LANES : (i + 1) * LANES].T
        for k in range(21):
            row_coef[k, i * LANES : (i + 1) * LANES, :] = jnp.broadcast_to(block[:, k : k + 1], (LANES, LANES))

    loads[1].wait()

    def send_block(f, s):
        for i in range(PIECES[s]):
            rung_copy(f, s, i).start()

    def field_steps(f, carry):
        for s in range(STEPS):
            for i in range(PIECES[s]):
                rung_copy(f, s, i).wait_recv()
                pl.when(has_fwd)(lambda: rail_copy(f, s, i).start())
                pass_tile(f, s, i)
            if s + AHEAD < STEPS:
                send_block(f, s + AHEAD)
            else:
                pl.when(f == 0)(lambda: send_block(1, s + AHEAD - STEPS))
            if s == 3:
                pl.when(f == 0)(lambda: own_columns(1))
            if s == 0:
                pl.when(f == 1)(lambda: finish(0))
            tasks(f, s)
        return carry

    lax.fori_loop(0, 2, field_steps, 0)
    finish(1)

    def drain(f, carry):
        for s in range(STEPS):
            for i in range(PIECES[s]):
                rung_copy(f, s, i).wait_send()
                pl.when(has_fwd)(lambda: rail_copy(f, s, i).wait_send())
        for side in range(2):
            for far in range(2):
                for half in range(2):
                    tile_copy(f, side, far, half, 2 * T, (r, c)).wait_send()
            _, edge = sides[side]
            first = even + edge.astype(jnp.int32) * (odd - even)
            corner_copy(f, side, first, 2 * T, (r, c)).wait_send()
            pl.when(has_b)(lambda: corner_copy(f, side, 1 - first, 2 * T, (r, c)).wait_send())
        return carry

    lax.fori_loop(0, 2, drain, 0)


def store_kernel(fin, g_out, c_out, sem):
    copies = [pltpu.make_async_copy(fin.at[k], out, sem.at[k]) for k, out in enumerate((g_out, c_out))]
    for copy in copies:
        copy.start()
    for copy in copies:
        copy.wait()


def shards(tile, n_rows, n_cols, group, g_start, cotangent, damping, hopping, bonds, source):
    T = tile
    block = jax.ShapeDtypeStruct(g_start.shape, jnp.float32)
    sems = 2 * (STEPS + EXTRA) + 12
    anywhere = pl.BlockSpec(memory_space=pl.ANY)
    fin = pl.pallas_call(
        functools.partial(kernel, T, n_rows, n_cols, group),
        out_shape=pltpu.VMEM((2,) + g_start.shape, jnp.float32),
        in_specs=[anywhere] * 6,
        out_specs=pl.BlockSpec(memory_space=pltpu.VMEM),
        scratch_shapes=[
            pltpu.VMEM((2, 6 * T, 8 * T), jnp.float32),
            pltpu.VMEM((4 * T, 6 * T), jnp.float32),
            pltpu.VMEM((21, 4 * T, LANES), jnp.float32),
            pltpu.VMEM((16, 6 * T), jnp.float32),
            pltpu.VMEM((LANES, 4 * T), jnp.float32),
            pltpu.VMEM((1, 14 * T), jnp.float32),
            pltpu.VMEM((6, 14 * T), jnp.float32),
            pltpu.VMEM((7, 14 * T), jnp.int32),
            pltpu.VMEM((7, 14 * T), jnp.float32),
            pltpu.VMEM((8, 14 * T), jnp.float32),
            pltpu.SemaphoreType.DMA((2,)),
            pltpu.SemaphoreType.DMA((4, 5)),
            pltpu.SemaphoreType.DMA((2, sems)),
            pltpu.SemaphoreType.DMA((2, sems)),
        ],
        compiler_params=pltpu.CompilerParams(
            collective_id=0, has_side_effects=True, vmem_limit_bytes=55 * 2**20
        ),
    )(g_start, cotangent, damping.reshape(1, -1), hopping, bonds, source)
    return pl.pallas_call(
        store_kernel,
        out_shape=(block, block),
        in_specs=[pl.BlockSpec(memory_space=pltpu.VMEM)],
        out_specs=(anywhere, anywhere),
        scratch_shapes=[pltpu.SemaphoreType.DMA((2,))],
        compiler_params=pltpu.CompilerParams(vmem_limit_bytes=2**20),
    )(fin)


def build(mesh, tile):
    n_rows = mesh.shape["row"]
    n_cols = mesh.shape["col"]
    return jax.shard_map(
        functools.partial(shards, tile, n_rows, n_cols, n_cols // 2),
        mesh=mesh,
        in_specs=(P("row", "col"), P("row", "col"), P(), P(), P(), P()),
        out_specs=(P("row", "col"), P("row", "col")),
        check_vma=False,
    )


def solution(mesh):
    return build(mesh, 2 * LX)
```

```python
import functools

import jax
import jax.numpy as jnp
from jax import lax
from jax.experimental import pallas as pl
from jax.experimental.pallas import tpu as pltpu
from jax.sharding import PartitionSpec as P

LX = 128
DT = 0.1
MESH = pl.DeviceIdType.MESH
STEPS = 8
AHEAD = 3
PIECES = (4, 2, 2, 2, 2, 2, 2, 4)
EXTRA = sum(PIECES) - STEPS
CHUNK = 32
LANES = 128


def band_offsets(side):
    return (0, 1, -1, 2, -2, 2 * side, -2 * side)


MIRROR = (0, 2, 1, 4, 3, 6, 5)


def kernel(
    tile,
    n_rows,
    n_cols,
    group,
    g_hbm,
    c_hbm,
    damping,
    hopping,
    bonds,
    source,
    fin,
    ext,
    mid,
    row_coef,
    col_tab,
    row_tab,
    win_damping,
    win_hopping,
    win_bonds,
    win_source,
    win_coef,
    load_sem,
    win_sem,
    send_sem,
    recv_sem,
):
    T = tile
    offsets = band_offsets(T // 2)
    modes = 4 * T * n_cols
    r = lax.axis_index("row")
    c = lax.axis_index("col")
    odd = lax.rem(r, 2)
    even = 1 - odd
    partner = r + 1 - 2 * odd
    other = r - 1 + 2 * odd
    has_b = jnp.logical_and(other >= 0, other < n_rows)
    fwd_row = r + 2 - 4 * odd
    has_fwd = jnp.logical_and(fwd_row >= 0, fwd_row < n_rows)
    src_row = r - 2 + 4 * odd
    left = lax.rem(c + n_cols - 1, n_cols)
    right = lax.rem(c + 1, n_cols)
    left_edge = lax.rem(c, group) == 0
    right_edge = lax.rem(c, group) == group - 1
    sides = ((left, left_edge), (right, right_edge))

    def row_at(p):
        return T * (odd * (4 - p) + even * (1 + p))

    a_heavy = row_at(3)
    b_heavy = row_at(0)
    half_a = even
    half_b = odd

    def aligned(value, step=None):
        return pl.multiple_of(value, T if step is None else step)

    def box(f, row, col, rows=T):
        return ext.at[f, pl.ds(aligned(row, rows), rows), pl.ds(aligned(col), T)]

    def remote(src, dst, f, index, to):
        return pltpu.make_async_remote_copy(
            src_ref=src,
            dst_ref=dst,
            send_sem=send_sem.at[f, index],
            recv_sem=recv_sem.at[f, index],
            device_id=to,
            device_id_type=MESH,
        )

    def order(s):
        return (3 * (s % 4)) % 4, s // 4

    def piece_of(s, i):
        rows = T // PIECES[s]
        return rows, i * rows, sum(PIECES[:s]) + i

    def rung_copy(f, s, i, src=None):
        q, heavy = order(s)
        rows, first, index = piece_of(s, i)
        half = odd * (1 - heavy) + even * heavy
        there = odd * (5 * T - heavy * T) + even * heavy * T
        if src is None:
            src = box(f, 2 * T + half * T + first, 2 * T + q * T, rows)
        else:
            src = src.at[pl.ds(aligned(half * T + first, rows), rows), pl.ds(q * T, T)]
        return remote(src, box(f, there + first, 2 * T + q * T, rows), f, index, (partner, c))

    def arrived_row(heavy):
        return odd * heavy * T + even * (5 * T - heavy * T)

    def rail_copy(f, s, i):
        q, heavy = order(s)
        rows, first, index = piece_of(s, i)
        there = odd * (4 * T + heavy * T) + even * (T - heavy * T)
        return remote(
            box(f, arrived_row(heavy) + first, 2 * T + q * T, rows),
            box(f, there + first, 2 * T + q * T, rows),
            f,
            STEPS + EXTRA + index,
            (fwd_row, c),
        )

    def wait_rail(f, s):
        @pl.when(has_b)
        def _():
            for i in range(PIECES[s]):
                rail_copy(f, s, i).wait_recv()

    def side_index(side, message):
        return 2 * (STEPS + EXTRA) + 6 * side + message

    def there_col(side, far):
        return (6 * T + far * T) if side == 0 else (T - far * T)

    def here_col(side, far):
        return (2 * T + far * T) if side == 0 else (5 * T - far * T)

    def tile_copy(f, side, far, half, row, to, rows=T, first=0):
        return remote(
            box(f, row + first, here_col(side, far), rows),
            box(f, 2 * T + half * T + first, there_col(side, far), rows),
            f,
            side_index(side, 2 * far + half),
            to,
        )

    def corner_copy(f, side, down, row, to):
        return remote(
            box(f, row, here_col(side, 0)),
            box(f, T + 3 * T * down, there_col(side, 0)),
            f,
            side_index(side, 4 + down),
            to,
        )

    def own_columns(f):
        for side, (col, edge) in enumerate(sides):
            @pl.when(jnp.logical_not(edge))
            def _():
                for far in range(2):
                    for half in range(2):
                        tile_copy(f, side, far, half, 2 * T + half * T, (r, col)).start()

            @pl.when(edge)
            def _():
                corner_copy(f, side, odd, 2 * T + even * T, (partner, col)).start()

                @pl.when(has_b)
                def _():
                    corner_copy(f, side, even, 2 * T + odd * T, (other, col)).start()

    def pass_tile(f, s, i):
        rows, first, _ = piece_of(s, i)
        q = (3 * (s % 4)) % 4
        heavy = s // 4
        side = 0 if q < 2 else 1
        far = 1 if q in (1, 2) else 0
        col, edge = sides[side]

        @pl.when(edge)
        def _():
            half = odd * heavy + even * (1 - heavy)
            tile_copy(f, side, far, half, arrived_row(heavy), (partner, col), rows, first).start()

    def pass_a_corner(f, side):
        col, edge = sides[side]

        @pl.when(jnp.logical_not(edge))
        def _():
            corner_copy(f, side, even, a_heavy, (r, col)).start()

    def pass_b_corner(f, side):
        col, edge = sides[side]

        @pl.when(jnp.logical_and(has_b, jnp.logical_not(edge)))
        def _():
            corner_copy(f, side, odd, b_heavy, (r, col)).start()

    def wait_tile(f, side, far, half):
        tile_copy(f, 1 - side, far, half, 2 * T, (r, c)).wait_recv()

    def wait_a_corner(f, side):
        corner_copy(f, 1 - side, even, 2 * T, (r, c)).wait_recv()

    def wait_b_corner(f, side):
        @pl.when(has_b)
        def _():
            corner_copy(f, 1 - side, odd, 2 * T, (r, c)).wait_recv()

    def spread_lanes(band):
        return jnp.concatenate([band] * (T // LANES), axis=1)

    def rate(f, src, row, col, coef_row, col_bands):
        wide = src[pl.ds(row, CHUNK), pl.ds(aligned(col - LANES, LANES), T + 2 * LANES)]
        tall = src[pl.ds(aligned(row - 8, 8), CHUNK + 16), pl.ds(col, T)]

        def rows_of(k):
            return spread_lanes(row_coef[7 * f + k, pl.ds(coef_row, CHUNK), :])

        total = tall[8 : 8 + CHUNK] * (rows_of(0) + col_bands[0])
        for k, offset in enumerate(offsets):
            if k == 0:
                continue
            if abs(offset) < 8:
                by_row = pltpu.roll(tall, (-offset) % (CHUNK + 16), 0)[8 : 8 + CHUNK]
                by_col = pltpu.roll(wide, (-offset) % (T + 2 * LANES), 1)[:, LANES : LANES + T]
            else:
                by_row = src[pl.ds(aligned(row + offset, CHUNK), CHUNK), pl.ds(col, T)]
                by_col = src[pl.ds(row, CHUNK), pl.ds(aligned(col + offset), T)]
            total = total + rows_of(k) * by_row + col_bands[k] * by_col
        return total

    def bands_at(f, b):
        block = col_tab[pl.ds(aligned(f * 8, 8), 8), pl.ds(aligned((b + 1) * T), T)]
        return [jnp.broadcast_to(block[k : k + 1], (CHUNK, T)) for k in range(7)]

    def add_source(f, dst, row, col, coef_row, b, scale):
        tiles = n_cols * 4
        shift = lax.rem(4 * c + b - 2 * r - (coef_row // T - 1) + 2 * tiles + 1, tiles)

        @pl.when(jnp.logical_and(f == 0, shift <= 2))
        def _():
            def body(i, carry):
                here = lax.broadcasted_iota(jnp.int32, (CHUNK, T), 1) - lax.broadcasted_iota(
                    jnp.int32, (CHUNK, T), 0
                )
                here = here + (shift - 1) * T - i * CHUNK
                at = pl.ds(aligned(row + i * CHUNK, CHUNK), CHUNK)
                total = dst[at, pl.ds(col, T)]
                for k, offset in enumerate(offsets):
                    feed = row_coef[14 + k, pl.ds(aligned(coef_row + i * CHUNK, CHUNK), CHUNK), :]
                    total = total + jnp.where(here == offset, spread_lanes(scale * feed), 0.0)
                dst[at, pl.ds(col, T)] = total
                return carry

            lax.fori_loop(0, T // CHUNK, body, 0)

    def mid_tile(f, row, b):
        row = aligned(row)
        col = aligned((b + 2) * T)
        inner = aligned((b + 1) * T)
        col_bands = bands_at(f, b)
        field = ext.at[f]
        target = mid.at[f]

        def body(i, carry):
            at = aligned(row + i * CHUNK, CHUNK)
            low = aligned(row - T + i * CHUNK, CHUNK)
            total = rate(f, field, at, col, low, col_bands)
            total = total + field[pl.ds(at, CHUNK), pl.ds(col, T)]
            target[pl.ds(low, CHUNK), pl.ds(inner, T)] = total
            return carry

        lax.fori_loop(0, T // CHUNK, body, 0, unroll=True)
        add_source(f, target, aligned(row - T), inner, aligned(row - T), b, 1.0)

    def mids(f, jobs):
        packed = sum((8 * p + b + 1) << (5 * i) for i, (p, b) in enumerate(jobs))

        def body(_, rest):
            p = lax.rem(rest, 32) // 8
            b = lax.rem(rest, 8) - 1

            @pl.when(jnp.logical_or(p > 0, has_b))
            def _():
                mid_tile(f, row_at(p), b)

            return rest // 32

        lax.fori_loop(0, len(jobs), body, jnp.int32(packed))

    def out_tile(f, half, b):
        col_bands = bands_at(f, b)
        col = aligned((b + 1) * T)
        outer = aligned((b + 2) * T)
        own = aligned(b * T)
        field = ext.at[f]
        done = fin.at[f]
        base = aligned(half * T)

        def body(i, carry):
            at = aligned(base + i * CHUNK, CHUNK)
            inner = aligned(base + T + i * CHUNK, CHUNK)
            total = rate(f, mid.at[f], inner, col, inner, col_bands)
            total = field[pl.ds(aligned(base + 2 * T + i * CHUNK, CHUNK), CHUNK), pl.ds(outer, T)] + 2.0 * total
            done[pl.ds(at, CHUNK), pl.ds(own, T)] = total
            return carry

        lax.fori_loop(0, T // CHUNK, body, 0, unroll=True)
        add_source(f, done, base, own, aligned(base + T), b, 2.0)

    def outs(f, jobs):
        packed = sum((4 * e + b) << (3 * i) for i, (e, b) in enumerate(jobs))

        def body(_, rest):
            e = lax.rem(rest, 8) // 4
            b = lax.rem(rest, 4)
            out_tile(f, (1 - e) * half_a + e * half_b, b)
            return rest // 8

        lax.fori_loop(0, len(jobs), body, jnp.int32(packed))

    def early(f, s, i):
        last = i == PIECES[s] - 1
        if s == 1 and last:
            wait_rail(f, 0)
            pass_b_corner(f, 0)
        if s == 2 and last:
            wait_rail(f, 1)
            pass_b_corner(f, 1)
            wait_tile(f, 0, 0, half_b)
            wait_tile(f, 1, 0, half_b)
            mids(f, ((1, 0), (1, 3)))
        if s == 4 and last:
            pass_a_corner(f, 0)
            wait_rail(f, 2)
            wait_rail(f, 3)
            mids(f, ((1, 2), (1, 1)))
        if s == 5 and last:
            pass_a_corner(f, 1)
            wait_rail(f, 4)
            wait_b_corner(f, 0)
            wait_b_corner(f, 1)
            wait_tile(f, 1, 0, half_a)
            wait_tile(f, 1, 1, half_b)
            mids(f, ((0, 0), (2, 3), (1, 4)))
        if s == 6 and last:
            wait_tile(f, 0, 0, half_a)
            wait_tile(f, 0, 1, half_b)
            mids(f, ((1, -1), (2, 0)))
        if s == 7 and i == 0:
            wait_rail(f, 5)
            mids(f, ((2, 2), (0, 3)))
        if s == 7 and i == 1:
            wait_a_corner(f, 1)
            mids(f, ((3, 3),))
        if s == 7 and i == 2:
            outs(f, ((1, 0), (1, 3)))

    def late(f, part):
        if part == 0:
            wait_a_corner(f, 0)
            mids(f, ((2, 1), (3, 0), (3, 1), (3, 2)))
        if part == 1:
            wait_rail(f, 6)
            mids(f, ((0, 2),))
            outs(f, ((0, 1), (0, 2), (1, 2)))
        if part == 2:
            wait_tile(f, 0, 1, half_a)
            wait_tile(f, 1, 1, half_a)
            mids(f, ((2, -1), (2, 4)))
            outs(f, ((0, 0), (0, 3)))
        if part == 3:
            wait_rail(f, 7)
            mids(f, ((0, 1),))
            outs(f, ((1, 1),))

    late_at = {(1, 0): 0, (1, 1): 1, (2, 0): 2, (3, 0): 3}

    row_first = r * 2 * T
    col_first = c * 4 * T
    spans = (
        (0, row_first + modes - 2 * T, 2 * T),
        (2 * T, row_first, 4 * T),
        (6 * T, col_first + modes - 2 * T, 2 * T),
        (8 * T, col_first, 4 * T),
        (12 * T, col_first + 4 * T, 2 * T),
    )
    arrays = (
        (damping, win_damping),
        (hopping, win_hopping),
        (bonds, win_bonds),
        (source, win_source),
    )

    def window_copies():
        for k, (src, dst) in enumerate(arrays):
            for i, (at, first, count) in enumerate(spans):
                start = aligned(lax.rem(first, modes), 2 * T)
                yield pltpu.make_async_copy(
                    src.at[:, pl.ds(start, count)], dst.at[:, pl.ds(at, count)], win_sem.at[k, i]
                )

    loads = [
        pltpu.make_async_copy(src, ext.at[k, pl.ds(2 * T, 2 * T), pl.ds(2 * T, 4 * T)], load_sem.at[k])
        for k, src in enumerate((g_hbm, c_hbm))
    ]
    barrier = pltpu.get_barrier_semaphore()

    def greet(row, col):
        pl.semaphore_signal(barrier, inc=1, device_id=(row, col), device_id_type=MESH)

    greet(partner, c)
    both = has_b.astype(jnp.int32)
    pl.when(has_fwd)(lambda: greet(fwd_row, c))
    pl.when(has_b)(lambda: greet(src_row, c))
    for col, edge in sides:
        pl.when(jnp.logical_not(edge))(lambda: greet(r, col))
        pl.when(edge)(lambda: greet(partner, col))
        pl.when(jnp.logical_and(edge, has_b))(lambda: greet(other, col))
    edges = left_edge.astype(jnp.int32) + right_edge.astype(jnp.int32)
    peers = 3 + has_fwd.astype(jnp.int32) + both + edges * both

    for load in loads:
        load.start()
    for copy in window_copies():
        copy.start()

    pl.semaphore_wait(barrier, peers)
    for s in range(AHEAD):
        for i in range(PIECES[s]):
            rung_copy(0, s, i, g_hbm).start()
    loads[0].wait()
    own_columns(0)

    @pl.when(jnp.logical_not(has_b))
    def _():
        for k in range(2):
            ext[k, pl.ds(aligned(b_heavy), T), pl.ds(T, 6 * T)] = jnp.zeros((T, 6 * T), jnp.float32)
            mid[k, pl.ds(aligned(b_heavy - T), T), :] = jnp.zeros((T, 6 * T), jnp.float32)

    for copy in window_copies():
        copy.wait()
    half_step = 0.5 * DT
    present = win_bonds[...].astype(jnp.float32)
    win_coef[0:1, :] = -half_step * win_damping[...] * present[0:1]
    win_coef[1:7, :] = half_step * win_hopping[...] * present[1:7]
    win_coef[7:8, :] = jnp.zeros((1, 14 * T), jnp.float32)

    def adjoint(first, count):
        window = win_coef[:, first : first + count + 2 * T]
        rows = []
        for k, offset in enumerate(offsets):
            band = window[MIRROR[k] : MIRROR[k] + 1]
            rows.append(pltpu.roll(band, (-offset) % (count + 2 * T), 1)[:, T : T + count])
        return rows

    row_tab[...] = jnp.zeros_like(row_tab)
    row_tab[0:8, :] = win_coef[:, T : 5 * T]
    for k, band in enumerate(adjoint(0, 4 * T)):
        row_tab[7 + k : 8 + k, :] = band
    row_tab[14:21, :] = half_step * win_source[:, T : 5 * T]
    col_tab[0:8, :] = win_coef[:, 7 * T : 13 * T]
    for k, band in enumerate(adjoint(6 * T, 6 * T)):
        col_tab[8 + k : 9 + k, :] = band
    for i in range(4 * T // LANES):
        block = row_tab[:, i * LANES : (i + 1) * LANES].T
        for k in range(21):
            row_coef[k, i * LANES : (i + 1) * LANES, :] = jnp.broadcast_to(block[:, k : k + 1], (LANES, LANES))

    loads[1].wait()

    def send_block(f, s):
        for i in range(PIECES[s]):
            rung_copy(f, s, i).start()

    def field_steps(f, carry):
        for s in range(STEPS):
            for i in range(PIECES[s]):
                rung_copy(f, s, i).wait_recv()
                pl.when(has_fwd)(lambda: rail_copy(f, s, i).start())
                pass_tile(f, s, i)
                if i == PIECES[s] - 1:
                    if s + AHEAD < STEPS:
                        send_block(f, s + AHEAD)
                    else:
                        pl.when(f == 0)(lambda: send_block(1, s + AHEAD - STEPS))
                    if s == 3:
                        pl.when(f == 0)(lambda: own_columns(1))
                if (s, i) in late_at:
                    pl.when(f == 1)(lambda: late(0, late_at[s, i]))
                early(f, s, i)
        return carry

    lax.fori_loop(0, 2, field_steps, 0)
    for part in range(4):
        late(1, part)

    def drain(f, carry):
        for s in range(STEPS):
            for i in range(PIECES[s]):
                rung_copy(f, s, i).wait_send()
                pl.when(has_fwd)(lambda: rail_copy(f, s, i).wait_send())
        for side in range(2):
            for far in range(2):
                for half in range(2):
                    tile_copy(f, side, far, half, 2 * T, (r, c)).wait_send()
            _, edge = sides[side]
            first = even + edge.astype(jnp.int32) * (odd - even)
            corner_copy(f, side, first, 2 * T, (r, c)).wait_send()
            pl.when(has_b)(lambda: corner_copy(f, side, 1 - first, 2 * T, (r, c)).wait_send())
        return carry

    lax.fori_loop(0, 2, drain, 0)


def store_kernel(fin, g_out, c_out, sem):
    copies = [pltpu.make_async_copy(fin.at[k], out, sem.at[k]) for k, out in enumerate((g_out, c_out))]
    for copy in copies:
        copy.start()
    for copy in copies:
        copy.wait()


def shards(tile, n_rows, n_cols, group, g_start, cotangent, damping, hopping, bonds, source):
    T = tile
    block = jax.ShapeDtypeStruct(g_start.shape, jnp.float32)
    sems = 2 * (STEPS + EXTRA) + 12
    anywhere = pl.BlockSpec(memory_space=pl.ANY)
    fin = pl.pallas_call(
        functools.partial(kernel, T, n_rows, n_cols, group),
        out_shape=pltpu.VMEM((2,) + g_start.shape, jnp.float32),
        in_specs=[anywhere] * 6,
        out_specs=pl.BlockSpec(memory_space=pltpu.VMEM),
        scratch_shapes=[
            pltpu.VMEM((2, 6 * T, 8 * T), jnp.float32),
            pltpu.VMEM((2, 4 * T, 6 * T), jnp.float32),
            pltpu.VMEM((21, 4 * T, LANES), jnp.float32),
            pltpu.VMEM((16, 6 * T), jnp.float32),
            pltpu.VMEM((LANES, 4 * T), jnp.float32),
            pltpu.VMEM((1, 14 * T), jnp.float32),
            pltpu.VMEM((6, 14 * T), jnp.float32),
            pltpu.VMEM((7, 14 * T), jnp.int32),
            pltpu.VMEM((7, 14 * T), jnp.float32),
            pltpu.VMEM((8, 14 * T), jnp.float32),
            pltpu.SemaphoreType.DMA((2,)),
            pltpu.SemaphoreType.DMA((4, 5)),
            pltpu.SemaphoreType.DMA((2, sems)),
            pltpu.SemaphoreType.DMA((2, sems)),
        ],
        compiler_params=pltpu.CompilerParams(
            collective_id=0, has_side_effects=True, vmem_limit_bytes=56 * 2**20
        ),
    )(g_start, cotangent, damping.reshape(1, -1), hopping, bonds, source)
    return pl.pallas_call(
        store_kernel,
        out_shape=(block, block),
        in_specs=[pl.BlockSpec(memory_space=pltpu.VMEM)],
        out_specs=(anywhere, anywhere),
        scratch_shapes=[pltpu.SemaphoreType.DMA((2,))],
        compiler_params=pltpu.CompilerParams(vmem_limit_bytes=2**20),
    )(fin)


def build(mesh, tile):
    n_rows = mesh.shape["row"]
    n_cols = mesh.shape["col"]
    return jax.shard_map(
        functools.partial(shards, tile, n_rows, n_cols, n_cols // 2),
        mesh=mesh,
        in_specs=(P("row", "col"), P("row", "col"), P(), P(), P(), P()),
        out_specs=(P("row", "col"), P("row", "col")),
        check_vma=False,
    )


def solution(mesh):
    return build(mesh, 2 * LX)
```

```python
import functools

import jax
import jax.numpy as jnp
from jax import lax
from jax.experimental import pallas as pl
from jax.experimental.pallas import tpu as pltpu
from jax.sharding import PartitionSpec as P

LX = 128
DT = 0.1
MESH = pl.DeviceIdType.MESH
STEPS = 8
AHEAD = 3
PIECES = (4, 2, 2, 2, 2, 2, 2, 4)
STORES = 4
EXTRA = sum(PIECES) - STEPS
CHUNK = 32
LANES = 128


def band_offsets(side):
    return (0, 1, -1, 2, -2, 2 * side, -2 * side)


MIRROR = (0, 2, 1, 4, 3, 6, 5)


def kernel(
    tile,
    n_rows,
    n_cols,
    group,
    g_hbm,
    c_hbm,
    damping,
    hopping,
    bonds,
    source,
    fin,
    ext,
    mid,
    row_coef,
    col_tab,
    row_tab,
    win_damping,
    win_hopping,
    win_bonds,
    win_source,
    win_coef,
    load_sem,
    win_sem,
    send_sem,
    recv_sem,
):
    T = tile
    offsets = band_offsets(T // 2)
    modes = 4 * T * n_cols
    r = lax.axis_index("row")
    c = lax.axis_index("col")
    odd = lax.rem(r, 2)
    even = 1 - odd
    partner = r + 1 - 2 * odd
    other = r - 1 + 2 * odd
    has_b = jnp.logical_and(other >= 0, other < n_rows)
    fwd_row = r + 2 - 4 * odd
    has_fwd = jnp.logical_and(fwd_row >= 0, fwd_row < n_rows)
    src_row = r - 2 + 4 * odd
    left = lax.rem(c + n_cols - 1, n_cols)
    right = lax.rem(c + 1, n_cols)
    left_edge = lax.rem(c, group) == 0
    right_edge = lax.rem(c, group) == group - 1
    sides = ((left, left_edge), (right, right_edge))

    def row_at(p):
        return T * (odd * (4 - p) + even * (1 + p))

    a_heavy = row_at(3)
    b_heavy = row_at(0)
    half_a = even
    half_b = odd

    def aligned(value, step=None):
        return pl.multiple_of(value, T if step is None else step)

    def box(f, row, col, rows=T):
        return ext.at[f, pl.ds(aligned(row, rows), rows), pl.ds(aligned(col), T)]

    def remote(src, dst, f, index, to):
        return pltpu.make_async_remote_copy(
            src_ref=src,
            dst_ref=dst,
            send_sem=send_sem.at[f, index],
            recv_sem=recv_sem.at[f, index],
            device_id=to,
            device_id_type=MESH,
        )

    def order(s):
        return (3 * (s % 4)) % 4, s // 4

    def piece_of(s, i):
        rows = T // PIECES[s]
        return rows, i * rows, sum(PIECES[:s]) + i

    def rung_copy(f, s, i, src=None):
        q, heavy = order(s)
        rows, first, index = piece_of(s, i)
        half = odd * (1 - heavy) + even * heavy
        there = odd * (5 * T - heavy * T) + even * heavy * T
        if src is None:
            src = box(f, 2 * T + half * T + first, 2 * T + q * T, rows)
        else:
            src = src.at[pl.ds(aligned(half * T + first, rows), rows), pl.ds(q * T, T)]
        return remote(src, box(f, there + first, 2 * T + q * T, rows), f, index, (partner, c))

    def arrived_row(heavy):
        return odd * heavy * T + even * (5 * T - heavy * T)

    def rail_copy(f, s, i):
        q, heavy = order(s)
        rows, first, index = piece_of(s, i)
        there = odd * (4 * T + heavy * T) + even * (T - heavy * T)
        return remote(
            box(f, arrived_row(heavy) + first, 2 * T + q * T, rows),
            box(f, there + first, 2 * T + q * T, rows),
            f,
            STEPS + EXTRA + index,
            (fwd_row, c),
        )

    def wait_rail(f, s):
        @pl.when(has_b)
        def _():
            for i in range(PIECES[s]):
                rail_copy(f, s, i).wait_recv()

    def side_index(side, message):
        return 2 * (STEPS + EXTRA) + 6 * side + message

    def there_col(side, far):
        return (6 * T + far * T) if side == 0 else (T - far * T)

    def here_col(side, far):
        return (2 * T + far * T) if side == 0 else (5 * T - far * T)

    def tile_copy(f, side, far, half, row, to, rows=T, first=0):
        return remote(
            box(f, row + first, here_col(side, far), rows),
            box(f, 2 * T + half * T + first, there_col(side, far), rows),
            f,
            side_index(side, 2 * far + half),
            to,
        )

    def corner_copy(f, side, down, row, to):
        return remote(
            box(f, row, here_col(side, 0)),
            box(f, T + 3 * T * down, there_col(side, 0)),
            f,
            side_index(side, 4 + down),
            to,
        )

    def own_columns(f):
        for side, (col, edge) in enumerate(sides):
            @pl.when(jnp.logical_not(edge))
            def _():
                for far in range(2):
                    for half in range(2):
                        tile_copy(f, side, far, half, 2 * T + half * T, (r, col)).start()

            @pl.when(edge)
            def _():
                corner_copy(f, side, odd, 2 * T + even * T, (partner, col)).start()

                @pl.when(has_b)
                def _():
                    corner_copy(f, side, even, 2 * T + odd * T, (other, col)).start()

    def pass_tile(f, s, i):
        rows, first, _ = piece_of(s, i)
        q = (3 * (s % 4)) % 4
        heavy = s // 4
        side = 0 if q < 2 else 1
        far = 1 if q in (1, 2) else 0
        col, edge = sides[side]

        @pl.when(edge)
        def _():
            half = odd * heavy + even * (1 - heavy)
            tile_copy(f, side, far, half, arrived_row(heavy), (partner, col), rows, first).start()

    def pass_a_corner(f, side):
        col, edge = sides[side]

        @pl.when(jnp.logical_not(edge))
        def _():
            corner_copy(f, side, even, a_heavy, (r, col)).start()

    def pass_b_corner(f, side):
        col, edge = sides[side]

        @pl.when(jnp.logical_and(has_b, jnp.logical_not(edge)))
        def _():
            corner_copy(f, side, odd, b_heavy, (r, col)).start()

    def wait_tile(f, side, far, half):
        tile_copy(f, 1 - side, far, half, 2 * T, (r, c)).wait_recv()

    def wait_a_corner(f, side):
        corner_copy(f, 1 - side, even, 2 * T, (r, c)).wait_recv()

    def wait_b_corner(f, side):
        @pl.when(has_b)
        def _():
            corner_copy(f, 1 - side, odd, 2 * T, (r, c)).wait_recv()

    def spread_lanes(band):
        return jnp.concatenate([band] * (T // LANES), axis=1)

    def rate(f, src, row, col, coef_row, col_bands):
        parts = [
            src[pl.ds(row, CHUNK), pl.ds(aligned(col + (q - 1) * LANES, LANES), LANES)] for q in range(T // LANES + 2)
        ]
        lane = lax.broadcasted_iota(jnp.int32, (CHUNK, LANES), 1)

        def shifted(offset):
            low = 1 if offset > 0 else 0
            turned = [pltpu.roll(part, (-offset) % LANES, 1) for part in parts[low : low + T // LANES + 1]]
            keep = lane < (-offset) % LANES
            return jnp.concatenate([jnp.where(keep, a, b) for a, b in zip(turned[:-1], turned[1:])], axis=1)

        tall = src[pl.ds(aligned(row - 8, 8), CHUNK + 16), pl.ds(col, T)]

        def rows_of(k):
            return spread_lanes(row_coef[7 * f + k, pl.ds(coef_row, CHUNK), :])

        total = tall[8 : 8 + CHUNK] * (rows_of(0) + col_bands[0])
        for k, offset in enumerate(offsets):
            if k == 0:
                continue
            if abs(offset) < 8:
                by_row = pltpu.roll(tall, (-offset) % (CHUNK + 16), 0)[8 : 8 + CHUNK]
                by_col = shifted(offset)
            else:
                by_row = src[pl.ds(aligned(row + offset, CHUNK), CHUNK), pl.ds(col, T)]
                by_col = src[pl.ds(row, CHUNK), pl.ds(aligned(col + offset), T)]
            total = total + rows_of(k) * by_row + col_bands[k] * by_col
        return total

    def bands_at(f, b):
        block = col_tab[pl.ds(aligned(f * 8, 8), 8), pl.ds(aligned((b + 1) * T), T)]
        return [jnp.broadcast_to(block[k : k + 1], (CHUNK, T)) for k in range(7)]

    def add_source(f, dst, row, col, coef_row, b, scale):
        tiles = n_cols * 4
        shift = lax.rem(4 * c + b - 2 * r - (coef_row // T - 1) + 2 * tiles + 1, tiles)

        @pl.when(jnp.logical_and(f == 0, shift <= 2))
        def _():
            def body(i, carry):
                here = lax.broadcasted_iota(jnp.int32, (CHUNK, T), 1) - lax.broadcasted_iota(
                    jnp.int32, (CHUNK, T), 0
                )
                here = here + (shift - 1) * T - i * CHUNK
                at = pl.ds(aligned(row + i * CHUNK, CHUNK), CHUNK)
                total = dst[at, pl.ds(col, T)]
                for k, offset in enumerate(offsets):
                    feed = row_coef[14 + k, pl.ds(aligned(coef_row + i * CHUNK, CHUNK), CHUNK), :]
                    total = total + jnp.where(here == offset, spread_lanes(scale * feed), 0.0)
                dst[at, pl.ds(col, T)] = total
                return carry

            lax.fori_loop(0, T // CHUNK, body, 0)

    def mid_tile(f, row, b):
        row = aligned(row)
        col = aligned((b + 2) * T)
        inner = aligned((b + 1) * T)
        col_bands = bands_at(f, b)
        field = ext.at[f]
        target = mid.at[f]

        def body(i, carry):
            at = aligned(row + i * CHUNK, CHUNK)
            low = aligned(row - T + i * CHUNK, CHUNK)
            total = rate(f, field, at, col, low, col_bands)
            total = total + field[pl.ds(at, CHUNK), pl.ds(col, T)]
            target[pl.ds(low, CHUNK), pl.ds(inner, T)] = total
            return carry

        lax.fori_loop(0, T // CHUNK, body, 0, unroll=True)
        add_source(f, target, aligned(row - T), inner, aligned(row - T), b, 1.0)

    def mids(f, jobs):
        packed = sum((8 * p + b + 1) << (5 * i) for i, (p, b) in enumerate(jobs))

        def body(_, rest):
            p = lax.rem(rest, 32) // 8
            b = lax.rem(rest, 8) - 1

            @pl.when(jnp.logical_or(p > 0, has_b))
            def _():
                mid_tile(f, row_at(p), b)

            return rest // 32

        lax.fori_loop(0, len(jobs), body, jnp.int32(packed))

    def out_tile(f, half, b):
        col_bands = bands_at(f, b)
        col = aligned((b + 1) * T)
        outer = aligned((b + 2) * T)
        own = aligned(b * T)
        field = ext.at[f]
        done = fin.at[f]
        base = aligned(half * T)

        def body(i, carry):
            at = aligned(base + i * CHUNK, CHUNK)
            inner = aligned(base + T + i * CHUNK, CHUNK)
            total = rate(f, mid.at[f], inner, col, inner, col_bands)
            total = field[pl.ds(aligned(base + 2 * T + i * CHUNK, CHUNK), CHUNK), pl.ds(outer, T)] + 2.0 * total
            done[pl.ds(at, CHUNK), pl.ds(own, T)] = total
            return carry

        lax.fori_loop(0, T // CHUNK, body, 0, unroll=True)
        add_source(f, done, base, own, aligned(base + T), b, 2.0)

    def outs(f, jobs):
        packed = sum((4 * e + b) << (3 * i) for i, (e, b) in enumerate(jobs))

        def body(_, rest):
            e = lax.rem(rest, 8) // 4
            b = lax.rem(rest, 4)
            out_tile(f, (1 - e) * half_a + e * half_b, b)
            return rest // 8

        lax.fori_loop(0, len(jobs), body, jnp.int32(packed))

    def early(f, s, i):
        last = i == PIECES[s] - 1
        if s == 1 and last:
            wait_rail(f, 0)
            pass_b_corner(f, 0)
        if s == 2 and last:
            wait_rail(f, 1)
            pass_b_corner(f, 1)
            wait_tile(f, 0, 0, half_b)
            wait_tile(f, 1, 0, half_b)
            mids(f, ((1, 0), (1, 3)))
        if s == 4 and last:
            pass_a_corner(f, 0)
            wait_rail(f, 2)
            wait_rail(f, 3)
            mids(f, ((1, 2), (1, 1)))
        if s == 5 and last:
            pass_a_corner(f, 1)
            wait_rail(f, 4)
            wait_b_corner(f, 0)
            wait_b_corner(f, 1)
            wait_tile(f, 1, 0, half_a)
            wait_tile(f, 1, 1, half_b)
            mids(f, ((0, 0), (2, 3), (1, 4)))
        if s == 6 and i == 0:
            wait_tile(f, 0, 0, half_a)
            wait_tile(f, 0, 1, half_b)
            mids(f, ((1, -1), (2, 0)))
        if s == 6 and last:
            wait_rail(f, 5)
            mids(f, ((2, 2), (0, 3)))
            outs(f, ((1, 0),))
        if s == 7 and i == 0:
            wait_a_corner(f, 1)
            mids(f, ((3, 3),))
            outs(f, ((1, 3),))
        if s == 7 and i == 1:
            wait_a_corner(f, 0)
            wait_tile(f, 0, 1, half_a)
            mids(f, ((2, -1),))
        if s == 7 and i == 2:
            wait_rail(f, 6)
            mids(f, ((0, 2),))
            outs(f, ((1, 2),))

    def late(f, part):
        if part == 0:
            mids(f, ((2, 1), (3, 0), (3, 1), (3, 2)))
        if part == 1:
            outs(f, ((0, 0), (0, 1), (0, 2)))
        if part == 2:
            wait_tile(f, 1, 1, half_a)
            mids(f, ((2, 4),))
            outs(f, ((0, 3),))
        if part == 3:
            wait_rail(f, 7)
            mids(f, ((0, 1),))
            outs(f, ((1, 1),))

    late_at = {(1, 0): 0, (1, 1): 1, (2, 0): 2, (3, 0): 3}

    row_first = r * 2 * T
    col_first = c * 4 * T
    spans = (
        (0, row_first + modes - 2 * T, 2 * T),
        (2 * T, row_first, 4 * T),
        (6 * T, col_first + modes - 2 * T, 2 * T),
        (8 * T, col_first, 4 * T),
        (12 * T, col_first + 4 * T, 2 * T),
    )
    arrays = (
        (damping, win_damping),
        (hopping, win_hopping),
        (bonds, win_bonds),
        (source, win_source),
    )

    def window_copies():
        for k, (src, dst) in enumerate(arrays):
            for i, (at, first, count) in enumerate(spans):
                start = aligned(lax.rem(first, modes), 2 * T)
                yield pltpu.make_async_copy(
                    src.at[:, pl.ds(start, count)], dst.at[:, pl.ds(at, count)], win_sem.at[k, i]
                )

    loads = [
        pltpu.make_async_copy(src, ext.at[k, pl.ds(2 * T, 2 * T), pl.ds(2 * T, 4 * T)], load_sem.at[k])
        for k, src in enumerate((g_hbm, c_hbm))
    ]
    barrier = pltpu.get_barrier_semaphore()

    def greet(row, col):
        pl.semaphore_signal(barrier, inc=1, device_id=(row, col), device_id_type=MESH)

    greet(partner, c)
    both = has_b.astype(jnp.int32)
    pl.when(has_fwd)(lambda: greet(fwd_row, c))
    pl.when(has_b)(lambda: greet(src_row, c))
    for col, edge in sides:
        pl.when(jnp.logical_not(edge))(lambda: greet(r, col))
        pl.when(edge)(lambda: greet(partner, col))
        pl.when(jnp.logical_and(edge, has_b))(lambda: greet(other, col))
    edges = left_edge.astype(jnp.int32) + right_edge.astype(jnp.int32)
    peers = 3 + has_fwd.astype(jnp.int32) + both + edges * both

    for load in loads:
        load.start()
    for copy in window_copies():
        copy.start()

    pl.semaphore_wait(barrier, peers)
    for s in range(AHEAD):
        for i in range(PIECES[s]):
            rung_copy(0, s, i, g_hbm).start()
    loads[0].wait()
    own_columns(0)

    @pl.when(jnp.logical_not(has_b))
    def _():
        for k in range(2):
            ext[k, pl.ds(aligned(b_heavy), T), pl.ds(T, 6 * T)] = jnp.zeros((T, 6 * T), jnp.float32)
            mid[k, pl.ds(aligned(b_heavy - T), T), :] = jnp.zeros((T, 6 * T), jnp.float32)

    for copy in window_copies():
        copy.wait()
    half_step = 0.5 * DT
    present = win_bonds[...].astype(jnp.float32)
    win_coef[0:1, :] = -half_step * win_damping[...] * present[0:1]
    win_coef[1:7, :] = half_step * win_hopping[...] * present[1:7]
    win_coef[7:8, :] = jnp.zeros((1, 14 * T), jnp.float32)

    def adjoint(first, count):
        window = win_coef[:, first : first + count + 2 * T]
        rows = []
        for k, offset in enumerate(offsets):
            band = window[MIRROR[k] : MIRROR[k] + 1]
            rows.append(pltpu.roll(band, (-offset) % (count + 2 * T), 1)[:, T : T + count])
        return rows

    row_tab[...] = jnp.zeros_like(row_tab)
    row_tab[0:8, :] = win_coef[:, T : 5 * T]
    for k, band in enumerate(adjoint(0, 4 * T)):
        row_tab[7 + k : 8 + k, :] = band
    row_tab[14:21, :] = half_step * win_source[:, T : 5 * T]
    col_tab[0:8, :] = win_coef[:, 7 * T : 13 * T]
    for k, band in enumerate(adjoint(6 * T, 6 * T)):
        col_tab[8 + k : 9 + k, :] = band
    for i in range(4 * T // LANES):
        block = row_tab[:, i * LANES : (i + 1) * LANES].T
        for k in range(21):
            row_coef[k, i * LANES : (i + 1) * LANES, :] = jnp.broadcast_to(block[:, k : k + 1], (LANES, LANES))

    loads[1].wait()

    def send_block(f, s):
        for i in range(PIECES[s]):
            rung_copy(f, s, i).start()

    def field_steps(f, carry):
        for s in range(STEPS):
            for i in range(PIECES[s]):
                rung_copy(f, s, i).wait_recv()
                pl.when(has_fwd)(lambda: rail_copy(f, s, i).start())
                pass_tile(f, s, i)
                if i == PIECES[s] - 1:
                    if s + AHEAD < STEPS:
                        send_block(f, s + AHEAD)
                    else:
                        pl.when(f == 0)(lambda: send_block(1, s + AHEAD - STEPS))
                    if s == 3:
                        pl.when(f == 0)(lambda: own_columns(1))
                if (s, i) in late_at:
                    pl.when(f == 1)(lambda: late(0, late_at[s, i]))
                early(f, s, i)
        return carry

    lax.fori_loop(0, 2, field_steps, 0)
    for part in range(4):
        late(1, part)

    def drain(f, carry):
        for s in range(STEPS):
            for i in range(PIECES[s]):
                rung_copy(f, s, i).wait_send()
                pl.when(has_fwd)(lambda: rail_copy(f, s, i).wait_send())
        for side in range(2):
            for far in range(2):
                for half in range(2):
                    tile_copy(f, side, far, half, 2 * T, (r, c)).wait_send()
            _, edge = sides[side]
            first = even + edge.astype(jnp.int32) * (odd - even)
            corner_copy(f, side, first, 2 * T, (r, c)).wait_send()
            pl.when(has_b)(lambda: corner_copy(f, side, 1 - first, 2 * T, (r, c)).wait_send())
        return carry

    lax.fori_loop(0, 2, drain, 0)


def store_kernel(fin, g_out, c_out, sem):
    rows = g_out.shape[0] // STORES
    copies = [
        pltpu.make_async_copy(fin.at[k, pl.ds(i * rows, rows)], out.at[pl.ds(i * rows, rows)], sem.at[k, i])
        for i in range(STORES)
        for k, out in enumerate((g_out, c_out))
    ]
    for copy in copies:
        copy.start()
    for copy in copies:
        copy.wait()


def shards(tile, n_rows, n_cols, group, g_start, cotangent, damping, hopping, bonds, source):
    T = tile
    block = jax.ShapeDtypeStruct(g_start.shape, jnp.float32)
    sems = 2 * (STEPS + EXTRA) + 12
    anywhere = pl.BlockSpec(memory_space=pl.ANY)
    fin = pl.pallas_call(
        functools.partial(kernel, T, n_rows, n_cols, group),
        out_shape=pltpu.VMEM((2,) + g_start.shape, jnp.float32),
        in_specs=[anywhere] * 6,
        out_specs=pl.BlockSpec(memory_space=pltpu.VMEM),
        scratch_shapes=[
            pltpu.VMEM((2, 6 * T, 8 * T), jnp.float32),
            pltpu.VMEM((2, 4 * T, 6 * T), jnp.float32),
            pltpu.VMEM((21, 4 * T, LANES), jnp.float32),
            pltpu.VMEM((16, 6 * T), jnp.float32),
            pltpu.VMEM((LANES, 4 * T), jnp.float32),
            pltpu.VMEM((1, 14 * T), jnp.float32),
            pltpu.VMEM((6, 14 * T), jnp.float32),
            pltpu.VMEM((7, 14 * T), jnp.int32),
            pltpu.VMEM((7, 14 * T), jnp.float32),
            pltpu.VMEM((8, 14 * T), jnp.float32),
            pltpu.SemaphoreType.DMA((2,)),
            pltpu.SemaphoreType.DMA((4, 5)),
            pltpu.SemaphoreType.DMA((2, sems)),
            pltpu.SemaphoreType.DMA((2, sems)),
        ],
        compiler_params=pltpu.CompilerParams(
            collective_id=0, has_side_effects=True, vmem_limit_bytes=56 * 2**20
        ),
    )(g_start, cotangent, damping.reshape(1, -1), hopping, bonds, source)
    return pl.pallas_call(
        store_kernel,
        out_shape=(block, block),
        in_specs=[pl.BlockSpec(memory_space=pltpu.VMEM)],
        out_specs=(anywhere, anywhere),
        scratch_shapes=[pltpu.SemaphoreType.DMA((2, STORES))],
        compiler_params=pltpu.CompilerParams(vmem_limit_bytes=2**20),
    )(fin)


def build(mesh, tile):
    n_rows = mesh.shape["row"]
    n_cols = mesh.shape["col"]
    return jax.shard_map(
        functools.partial(shards, tile, n_rows, n_cols, n_cols // 2),
        mesh=mesh,
        in_specs=(P("row", "col"), P("row", "col"), P(), P(), P(), P()),
        out_specs=(P("row", "col"), P("row", "col")),
        check_vma=False,
    )


def solution(mesh):
    return build(mesh, 2 * LX)
```
